32 devices in a mesh: ta: 4 (over y, x), ha: 2 (over core), head: 4 (over z).
Axes of the slice: x: 2, y: 2, z: 4, core: 2. Of those that a mesh axis runs over, the one named last changes fastest.
Arguments:
- queries: bfloat16 [24, 16, 8, 2048], P('ta', ('ha', 'head')), may hold values from -90 to 90
- keys: bfloat16 [24, 16, 8, 2048], P('ta', ('ha', 'head')), may hold values from -4.5 to 4.5
- values: bfloat16 [24, 16, 8, 2048], P('ta', ('ha', 'head')), may hold values from -6 to 6
- out_grad: bfloat16 [24, 16, 8, 2048], P('ta', ('ha', 'head')), may hold values from -6 to 6
Outputs:
- attended: bfloat16 [24, 16, 8, 2048], P('ta', ('ha', 'head'))
- query_grad: bfloat16 [24, 16, 8, 2048], P('ta', ('ha', 'head'))
- key_grad: bfloat16 [24, 16, 8, 2048], P('ta', ('ha', 'head'))
- value_grad: bfloat16 [24, 16, 8, 2048], P('ta', ('ha', 'head'))
The draws below stay inside these ranges and needn't reach their ends.
All inputs are finite; a program needn't handle non-finite values.
Results may differ from the reference program's by a relative error of at most 0.025.
Values may be sent and summed in bfloat16 or wider, within the bound.
A program may use at most 128 MiB of HBM per device.

```python
import math
import jax
import jax.numpy as jnp
from jax import lax

TT = 6
TH = 8
W = 8
HEADS = 16
DH = 128
NT = 24
NH = 16
CH = 2048


def pair_draw(key):
    shape = (NT * NH * W, CH)
    key_flat = jnp.clip(jax.random.normal(jax.random.fold_in(key, 21), shape, jnp.float32), -4.0, 4.0)
    query_flat = jnp.clip(jax.random.normal(jax.random.fold_in(key, 22), shape, jnp.float32), -4.0, 4.0)
    return (query_flat.reshape(NT, NH, W, CH), key_flat.reshape(NT, NH, W, CH))


def draw_queries(key, part):
    return pair_draw(key)[0].astype(jnp.bfloat16)


def draw_keys(key, part):
    return pair_draw(key)[1].astype(jnp.bfloat16)


def shard_levels(stream_key, shape, split, least, largest):
    loudness, own = 1.0, jax.random.fold_in(stream_key, 6)
    for dim, shards_of in split:
        heights = jnp.exp(jax.random.uniform(jax.random.fold_in(own, dim), (shards_of,), jnp.float32, least / len(split), largest / len(split)))
        loudness = loudness * jnp.repeat(heights, shape[dim] // shards_of).reshape([-1 if axis == dim else 1 for axis in range(len(shape))])
    return loudness


def gaussian(key, shape, spread, limit, pieces=(), kind=jnp.bfloat16):
    values = jax.random.normal(key, shape, jnp.float32) * spread
    if len(pieces) > 0:
        values = shard_levels(key, shape, pieces, -0.22, 0.18) * values
    return jnp.clip(values, min=-limit, max=limit).astype(kind)


def setup_inputs(seed: int = 0) -> dict:
    key_of = jax.random.split(jax.random.key(seed), 5)
    return {
        "queries": draw_queries(jax.random.fold_in(key_of[4], 71), 0),
        "keys": draw_keys(jax.random.fold_in(key_of[4], 71), 0),
        "values": gaussian(key_of[2], (NT, NH, W, CH), 1.0, 6.0, ((0, 4), (1, 8))),
        "out_grad": gaussian(key_of[3], (NT, NH, W, CH), 1.0, 6.0, ((0, 4), (1, 8))),
    }


def to_blocks(array, count_t, count_h, columns):
    shaped = array.reshape(count_t, TT, count_h, TH, columns, HEADS, DH)
    return shaped.transpose(0, 2, 5, 1, 3, 4, 6).reshape(count_t, count_h, HEADS, TT * TH * columns, DH)

def from_blocks(array, count_t, count_h, columns):
    shaped = array.reshape(count_t, count_h, HEADS, TT, TH, columns, DH)
    return shaped.transpose(0, 3, 1, 4, 5, 2, 6).reshape(count_t * TT, count_h * TH, columns, HEADS * DH)

def pad_tiles(array):
    return jnp.pad(array, ((1, 1), (1, 1)) + ((0, 0),) * (array.ndim - 2))

def beside_all(padded, first, second):
    zero = jnp.zeros((), jnp.int32)
    starts = (first.astype(jnp.int32), second.astype(jnp.int32)) + (zero,) * (padded.ndim - 2)
    sizes = (3, 3) + padded.shape[2:]
    piece = lax.dynamic_slice(padded, starts, sizes)
    moved = jnp.moveaxis(piece, 2, 0)
    return moved.reshape((HEADS, 9 * padded.shape[3]) + padded.shape[4:])

def window(first, second, count_t, count_h, tokens):
    offsets = jnp.arange(3, dtype=jnp.int32) - 1
    time_valid = (first + offsets >= 0) & (first + offsets < count_t)
    row_valid = (second + offsets >= 0) & (second + offsets < count_h)
    key_valid = jnp.repeat((time_valid[:, None] & row_valid[None, :]).reshape(9), tokens)
    return key_valid[None, :]

def reference(queries, keys, values, out_grad):
    count_t = queries.shape[0] // TT
    count_h = queries.shape[1] // TH
    columns = queries.shape[2]
    tokens = TT * TH * columns
    factor = 1.0 / math.sqrt(DH)
    query_blocks = to_blocks(queries, count_t, count_h, columns)
    key_blocks = to_blocks(keys, count_t, count_h, columns)
    value_blocks = to_blocks(values, count_t, count_h, columns)
    grad_blocks = to_blocks(out_grad, count_t, count_h, columns)
    key_pad = pad_tiles(key_blocks)
    value_pad = pad_tiles(value_blocks)

    def forward(index):
        first = index // count_h
        second = index % count_h
        allowed = window(first, second, count_t, count_h, tokens)
        own_q = query_blocks[first, second].astype(jnp.float32)
        own_g = grad_blocks[first, second].astype(jnp.float32)
        near_k = beside_all(key_pad, first, second).astype(jnp.float32)
        near_v = beside_all(value_pad, first, second).astype(jnp.float32)
        scores = jnp.einsum('hqd,hkd->hqk', own_q, near_k) * factor
        scores = jnp.where(allowed[None], scores, -jnp.inf)
        highest = lax.optimization_barrier(jnp.max(scores, axis=2, keepdims=True))
        log_total = highest + jnp.log(lax.optimization_barrier(jnp.sum(jnp.exp(scores - highest), axis=2, keepdims=True)))
        probs = jnp.where(allowed[None], jnp.exp(scores - log_total), 0.0)
        probs_low = probs.astype(jnp.bfloat16).astype(jnp.float32)
        attended = jnp.einsum('hqk,hkd->hqd', probs_low, near_v).astype(jnp.bfloat16)
        row_dot = lax.optimization_barrier(jnp.sum(own_g * attended.astype(jnp.float32), axis=2))
        prob_grad = jnp.einsum('hqd,hkd->hqk', own_g, near_v)
        score_grad = (probs * (prob_grad - row_dot[:, :, None])).astype(jnp.bfloat16).astype(jnp.float32)
        query_grad = (jnp.einsum('hqk,hkd->hqd', score_grad, near_k) * factor).astype(jnp.bfloat16)
        return (attended, log_total[:, :, 0], row_dot, query_grad)
    indices = jnp.arange(count_t * count_h, dtype=jnp.int32)
    attended, log_total, row_dot, query_grad = lax.map(forward, indices)
    query_pad = pad_tiles(query_blocks)
    grad_pad = pad_tiles(grad_blocks)
    total_pad = pad_tiles(log_total.reshape(count_t, count_h, HEADS, tokens))
    dot_pad = pad_tiles(row_dot.reshape(count_t, count_h, HEADS, tokens))

    def backward(index):
        first = index // count_h
        second = index % count_h
        allowed_back = window(first, second, count_t, count_h, tokens).T
        own_k = key_blocks[first, second].astype(jnp.float32)
        own_v = value_blocks[first, second].astype(jnp.float32)
        near_q = beside_all(query_pad, first, second).astype(jnp.float32)
        near_g = beside_all(grad_pad, first, second).astype(jnp.float32)
        near_total = beside_all(total_pad, first, second)
        near_dot = beside_all(dot_pad, first, second)
        scores = jnp.einsum('hqd,hkd->hqk', near_q, own_k) * factor
        probs = jnp.where(allowed_back[None], jnp.exp(scores - near_total[:, :, None]), 0.0)
        probs_low = probs.astype(jnp.bfloat16).astype(jnp.float32)
        value_grad = jnp.einsum('hqk,hqd->hkd', probs_low, near_g).astype(jnp.bfloat16)
        prob_grad = jnp.einsum('hqd,hkd->hqk', near_g, own_v)
        score_grad = (probs * (prob_grad - near_dot[:, :, None])).astype(jnp.bfloat16).astype(jnp.float32)
        key_grad = (jnp.einsum('hqk,hqd->hkd', score_grad, near_q) * factor).astype(jnp.bfloat16)
        return (key_grad, value_grad)
    key_grad, value_grad = lax.map(backward, indices)
    shape_back = (count_t, count_h, HEADS, tokens, DH)
    return (from_blocks(attended.reshape(shape_back), count_t, count_h, columns), from_blocks(query_grad.reshape(shape_back), count_t, count_h, columns), from_blocks(key_grad.reshape(shape_back), count_t, count_h, columns), from_blocks(value_grad.reshape(shape_back), count_t, count_h, columns))
```

```python
import functools
import math

import jax
import jax.numpy as jnp
from jax import lax
from jax.experimental import pallas as pl
from jax.experimental.pallas import tpu as pltpu
from jax.sharding import PartitionSpec as P

DH = 128
LOW = -1e30
MESH = pl.DeviceIdType.MESH


def sides_of(axis, size):
    me = lax.axis_index(axis)
    if size == 1:
        return []
    if size == 2:
        return [(1 - me, None, 1)]
    return [(me - 1, me > 0, 2), (me + 1, me < size - 1, 1)]


def guarded(valid, fn):
    if valid is None:
        fn()
    else:
        pl.when(valid)(fn)


def flip(index, bits):
    step = 1
    while step <= bits:
        if bits // step % 2:
            index = index + step - 2 * step * (lax.rem(lax.div(index, step), 2))
        step *= 2
    return index


def kernel(
    sizes,
    rows,
    heads,
    q_ref,
    k_ref,
    v_ref,
    g_ref,
    o_ref,
    dq_ref,
    dk_ref,
    dv_ref,
    qg,
    win,
    s_ref,
    outb,
    own,
    r1s,
    r1r,
    r2s,
    r2r,
    in_s,
    in_r,
    px_s,
    px_r,
    py_s,
    py_r,
    hc_s,
    hc_r,
    bc_s,
    bc_r,
    bx_s,
    bx_r,
    by_s,
    by_r,
    ou_s,
    ou_r,
):
    size_t, size_h, size_z = sizes
    tokens = rows * size_z
    z = lax.axis_index("head")
    ta = lax.axis_index("ta")
    corner = (ta == 0) | (ta == size_t - 1)
    inner = jnp.logical_not(corner)
    pair = flip(ta, 1)
    relay = size_t == 4
    across = flip(ta, 2) if relay else ta - 1 + 2 * lax.rem(ta, 2)
    sides = sides_of("ha", size_h)
    nt, nr = 3, 1 + len(sides)
    factor = 1.0 / math.sqrt(DH)
    scale = factor * math.log2(math.e)
    hops = list(range(size_z - 1, 0, -1))

    barrier = pltpu.get_barrier_semaphore()
    expected = size_z
    for d in hops:
        pl.semaphore_signal(barrier, inc=1, device_id={"head": flip(z, d)}, device_id_type=MESH)
    pl.semaphore_signal(barrier, inc=1, device_id={"ta": pair}, device_id_type=MESH)
    for axis, peer, valid in [("ta", across, None if relay else inner)] + [("ha", peer, valid) for peer, valid, _ in sides]:

        def greet(axis=axis, peer=peer):
            pl.semaphore_signal(barrier, inc=1, device_id={axis: peer}, device_id_type=MESH)

        guarded(valid, greet)
        expected = expected + (1 if valid is None else jnp.where(valid, 1, 0))
    pl.semaphore_wait(barrier, expected)

    def columns(group, h):
        return pl.ds(pl.multiple_of((group * heads + h) * DH, DH), DH)

    def part(group):
        return pl.ds(pl.multiple_of(group * rows, rows), rows)

    ins = (k_ref, v_ref, q_ref, g_ref)
    outs = (o_ref, dq_ref, dk_ref, dv_ref)

    def remote(src, dst, send, recv, device):
        return pltpu.make_async_remote_copy(
            src_ref=src, dst_ref=dst, send_sem=send, recv_sem=recv, device_id=device, device_id_type=MESH
        )

    def landing(h, a, group):
        if a < 2:
            return win.at[h, 0, 0, a, part(group), :]
        return qg.at[h, a - 2, part(group), :]

    def in_copy(h, a, d):
        peer = flip(z, d)
        return remote(ins[a].at[:, columns(peer, h)], landing(h, a, z), in_s.at[h, a, d], in_r.at[h, a, d], {"head": peer})

    def out_copy(h, a, d):
        peer = flip(z, d)
        return remote(outb.at[h, a, part(peer), :], outs[a].at[:, columns(z, h)], ou_s.at[h, a, d], ou_r.at[h, a, d], {"head": peer})

    def pair_copy(h, a):
        return remote(win.at[h, 0, 0, a], win.at[h, 0, 1, a], px_s.at[h, a], px_r.at[h, a], {"ta": pair})

    def across_copy(h, a):
        return remote(win.at[h, 0, 1 if relay else 0, a], win.at[h, 0, 2, a], py_s.at[h, a], py_r.at[h, a], {"ta": across})

    def side_copy(h, i, t):
        peer, _, there = sides[i]
        return remote(win.at[h, 0, t], win.at[h, there, t], hc_s.at[h, i, t], hc_r.at[h, there - 1, t], {"ha": peer})

    def back_side(h, i, t):
        peer, _, there = sides[i]
        return remote(r1s.at[h, i, t], r1r.at[h, there - 1, t], bc_s.at[h, i, t], bc_r.at[h, there - 1, t], {"ha": peer})

    def back_pair(h, a):
        return remote(r2s.at[h, 0, a], r2r.at[h, 0, a], bx_s.at[h, a], bx_r.at[h, a], {"ta": pair})

    def back_across(h, a):
        return remote(r2s.at[h, 1, a], r2r.at[h, 1, a], by_s.at[h, a], by_r.at[h, a], {"ta": across})

    def from_side(h, i, t):
        peer = sides[i][0]
        return remote(win.at[h, i + 1, t], win.at[h, i + 1, t], hc_r.at[h, i, t], hc_r.at[h, i, t], {"ha": peer})

    def back_from_side(h, i, t):
        peer = sides[i][0]
        return remote(r1r.at[h, i, t], r1r.at[h, i, t], bc_r.at[h, i, t], bc_r.at[h, i, t], {"ha": peer})

    def both(valid, other):
        return other if valid is None else valid & other

    def send_in(h):
        for a in range(4):
            for d in hops:
                in_copy(h, a, d).start()

    for h in range(min(2, heads)):
        send_in(h)

    @pl.when(corner)
    def _():
        @pl.loop(0, heads)
        def _(h):
            for r in range(nr):
                win[h, r, 2] = jnp.zeros((2, tokens, DH), win.dtype)

    for i, (peer, valid, _) in enumerate(sides):
        if valid is not None:

            @pl.when(jnp.logical_not(valid))
            def _(i=i):
                @pl.loop(0, heads)
                def _(h):
                    win[h, i + 1] = jnp.zeros((nt, 2, tokens, DH), win.dtype)

    @pl.loop(0, heads)
    def _(h):
        for a in range(4):
            landing(h, a, z)[...] = ins[a][:, columns(z, h)]

    def to_sides(h, t, cond=None):
        for i, (peer, valid, _) in enumerate(sides):
            go = valid if cond is None else both(valid, cond)
            guarded(go, lambda i=i: side_copy(h, i, t).start())

    def spread_own(h):
        for a in range(2):
            for d in hops:
                in_copy(h, a, d).wait_recv()
            pair_copy(h, a).start()
            if not relay:
                pl.when(inner)(lambda a=a: across_copy(h, a).start())
        to_sides(h, 0)

    def spread_pair(h):
        for a in range(2):
            pair_copy(h, a).wait_recv()
            if relay:
                pl.when(corner)(lambda a=a: across_copy(h, a).start())
        to_sides(h, 1)

    def spread_across(h):
        @pl.when(inner)
        def _():
            for a in range(2):
                across_copy(h, a).wait_recv()
            to_sides(h, 2)

    def score(h):
        for d in hops:
            in_copy(h, 2, d).wait_recv()
        queries = qg[h, 0]
        highest = jnp.full((1, tokens), LOW, jnp.float32)
        for r in range(nr):
            for t in range(nt):
                if r > 0:
                    valid = sides[r - 1][1]
                    guarded(both(valid, inner) if t == 2 else valid, lambda r=r, t=t: from_side(h, r - 1, t).wait_recv())
                scores = lax.dot_general(win[h, r, t, 0], queries, (((1,), (1,)), ((), ())), preferred_element_type=jnp.float32) * scale
                for cond in ([inner] if t == 2 else []) + ([sides[r - 1][1]] if r > 0 else []):
                    if cond is not None:
                        scores = jnp.where(cond, scores, LOW)
                s_ref[r * nt + t] = scores
                highest = jnp.maximum(highest, jnp.max(scores, axis=0, keepdims=True))
        return highest

    def forward(h, highest):
        for d in hops:
            in_copy(h, 3, d).wait_recv()
        grads = qg[h, 1]
        total = jnp.zeros((1, tokens), jnp.float32)
        mixed = jnp.zeros((DH, tokens), jnp.float32)
        for r in range(nr):
            for t in range(nt):
                weights = jnp.exp2(s_ref[r * nt + t] - highest)
                s_ref[r * nt + t] = weights
                total = total + jnp.sum(weights, axis=0, keepdims=True)
                mixed = mixed + lax.dot_general(
                    win[h, r, t, 1], weights.astype(jnp.bfloat16), (((0,), (0,)), ((), ())), preferred_element_type=jnp.float32
                )
        inverse = 1.0 / total
        attended = jnp.transpose(mixed * inverse).astype(jnp.bfloat16)
        outb[h, 0] = attended
        products = grads.astype(jnp.float32) * attended.astype(jnp.float32)
        row_dot = jnp.sum(jnp.transpose(products), axis=0, keepdims=True)
        for d in hops:
            out_copy(h, 0, d).start()
        return inverse, row_dot

    def backward(h, inverse, row_dot, query_grad, rs):
        queries = qg[h, 0]
        grads = qg[h, 1]
        for r in rs:
            for t in reversed(range(nt)):
                keys, values = win[h, r, t, 0], win[h, r, t, 1]
                probs = s_ref[r * nt + t] * inverse
                value_term = jnp.dot(probs.astype(jnp.bfloat16), grads, preferred_element_type=jnp.float32)
                prob_grad = lax.dot_general(values, grads, (((1,), (1,)), ((), ())), preferred_element_type=jnp.float32)
                score_grad = (probs * (prob_grad - row_dot)).astype(jnp.bfloat16)
                query_grad = query_grad + lax.dot_general(
                    keys, score_grad, (((0,), (0,)), ((), ())), preferred_element_type=jnp.float32
                )
                key_term = jnp.dot(score_grad, queries, preferred_element_type=jnp.float32) * factor
                if r == 0:
                    own[h, t, 0] = key_term
                    own[h, t, 1] = value_term
                else:
                    r1s[h, r - 1, t, 0] = key_term.astype(jnp.bfloat16)
                    r1s[h, r - 1, t, 1] = value_term.astype(jnp.bfloat16)
                    valid = sides[r - 1][1]
                    guarded(both(valid, inner) if t == 2 else valid, lambda r=r, t=t: back_side(h, r - 1, t).start())
        return query_grad

    def send_query_grad(h, query_grad):
        outb[h, 1] = jnp.transpose(query_grad * factor).astype(jnp.bfloat16)
        for d in hops:
            out_copy(h, 1, d).start()

    def fold_sides(h):
        for t in reversed(range(nt)):
            for i, (peer, valid, _) in enumerate(sides):

                def fold(i=i, t=t):
                    back_from_side(h, i, t).wait_recv()
                    own[h, t] = own[h, t] + r1r[h, i, t].astype(jnp.float32)

                guarded(both(valid, inner) if t == 2 else valid, fold)
            if t > 0:

                def send(t=t):
                    for a in range(2):
                        r2s[h, t - 1, a] = own[h, t, a].astype(jnp.bfloat16)
                        (back_across if t == 2 else back_pair)(h, a).start()

                guarded(inner if relay or t == 2 else None, send)

    def fold_across(h):
        @pl.when(corner if relay else inner)
        def _():
            for a in range(2):
                back_across(h, a).wait_recv()
                if relay:
                    r2s[h, 0, a] = (own[h, 1, a] + r2r[h, 1, a].astype(jnp.float32)).astype(jnp.bfloat16)
                    back_pair(h, a).start()
                else:
                    own[h, 0, a] = own[h, 0, a] + r2r[h, 1, a].astype(jnp.float32)

    def fold_pair(h):
        for a in range(2):
            back_pair(h, a).wait_recv()
            outb[h, a + 2] = (own[h, 0, a] + r2r[h, 0, a].astype(jnp.float32)).astype(jnp.bfloat16)
            for d in hops:
                out_copy(h, a + 2, d).start()
        for a in range(4):
            outs[a][:, columns(z, h)] = outb[h, a, part(z), :]

    def later(h, fn):
        pl.when(h < heads)(lambda: fn(h))

    def earlier(h, fn):
        pl.when(h >= 0)(lambda: fn(h))

    spread_own(0)
    later(jnp.int32(2), send_in)
    spread_pair(0)
    spread_across(0)

    @pl.loop(0, heads)
    def _(h):
        highest = score(h)
        later(h + 1, spread_own)
        later(h + 3, send_in)
        inverse, row_dot = forward(h, highest)
        earlier(h - 1, fold_across)
        query_grad = backward(h, inverse, row_dot, jnp.zeros((DH, tokens), jnp.float32), range(nr - 1, 0, -1))
        later(h + 1, spread_pair)
        query_grad = backward(h, inverse, row_dot, query_grad, (0,))
        send_query_grad(h, query_grad)
        earlier(h - 1, fold_pair)
        fold_sides(h)
        later(h + 1, spread_across)

    fold_across(heads - 1)
    fold_pair(heads - 1)

    @pl.loop(0, heads)
    def _(h):
        for a in range(4):
            for d in hops:
                in_copy(h, a, d).wait_send()
                out_copy(h, a, d).wait_recv()
                out_copy(h, a, d).wait_send()
        for a in range(2):
            pair_copy(h, a).wait_send()
            back_pair(h, a).wait_send()
            pl.when(corner if relay else inner)(lambda a=a: across_copy(h, a).wait_send())
            pl.when(inner)(lambda a=a: back_across(h, a).wait_send())
        for i, (peer, valid, _) in enumerate(sides):
            for t in range(nt):

                def drain(i=i, t=t):
                    side_copy(h, i, t).wait_send()
                    back_side(h, i, t).wait_send()

                guarded(both(valid, inner) if t == 2 else valid, drain)


def store(*refs):
    sems = refs[8]
    copies = [pltpu.make_async_copy(refs[i], refs[4 + i], sems.at[i]) for i in range(4)]
    for copy in copies:
        copy.start()
    for copy in copies:
        copy.wait()


def body(queries, keys, values, out_grad):
    sizes = tuple(lax.axis_size(axis) for axis in ("ta", "ha", "head"))
    size_t, size_h, size_z = sizes
    assert size_t % 2 == 0 and size_z & (size_z - 1) == 0
    shape = queries.shape
    rows = shape[0] * shape[1] * shape[2]
    width = shape[3]
    heads = width // DH // size_z
    tokens = rows * size_z
    nt, nr = 3, min(3, size_h)
    bf16 = jnp.bfloat16
    dma = pltpu.SemaphoreType.DMA
    mr = max(1, nr - 1)
    flat = [x.reshape(rows, width) for x in (queries, keys, values, out_grad)]
    outs = pl.pallas_call(
        functools.partial(kernel, sizes, rows, heads),
        out_shape=[jax.ShapeDtypeStruct((rows, width), bf16)] * 4,
        in_specs=[pl.BlockSpec(memory_space=pltpu.VMEM)] * 4,
        out_specs=[pl.BlockSpec(memory_space=pltpu.VMEM)] * 4,
        scratch_shapes=[
            pltpu.VMEM((heads, 2, tokens, DH), bf16),
            pltpu.VMEM((heads, nr, nt, 2, tokens, DH), bf16),
            pltpu.VMEM((nr * nt, tokens, tokens), jnp.float32),
            pltpu.VMEM((heads, 4, tokens, DH), bf16),
            pltpu.VMEM((heads, nt, 2, tokens, DH), jnp.float32),
            pltpu.VMEM((heads, mr, nt, 2, tokens, DH), bf16),
            pltpu.VMEM((heads, mr, nt, 2, tokens, DH), bf16),
            pltpu.VMEM((heads, 2, 2, tokens, DH), bf16),
            pltpu.VMEM((heads, 2, 2, tokens, DH), bf16),
            dma((heads, 4, size_z)),
            dma((heads, 4, size_z)),
            dma((heads, 2)),
            dma((heads, 2)),
            dma((heads, 2)),
            dma((heads, 2)),
            dma((heads, mr, nt)),
            dma((heads, mr, nt)),
            dma((heads, mr, nt)),
            dma((heads, mr, nt)),
            dma((heads, 2)),
            dma((heads, 2)),
            dma((heads, 2)),
            dma((heads, 2)),
            dma((heads, 4, size_z)),
            dma((heads, 4, size_z)),
        ],
        compiler_params=pltpu.CompilerParams(collective_id=0, has_side_effects=True, vmem_limit_bytes=56 * 1024 * 1024),
        name="tile_attention",
    )(*flat)
    outs = pl.pallas_call(
        store,
        out_shape=[jax.ShapeDtypeStruct((rows, width), bf16)] * 4,
        in_specs=[pl.BlockSpec(memory_space=pltpu.VMEM)] * 4,
        out_specs=[pl.BlockSpec(memory_space=pl.ANY)] * 4,
        scratch_shapes=[dma((4,))],
        name="store",
    )(*outs)
    return tuple(x.reshape(shape) for x in outs)


def solution(mesh):
    spec = P("ta", ("ha", "head"), None, None)
    return jax.shard_map(body, mesh=mesh, in_specs=(spec,) * 4, out_specs=(spec,) * 4, check_vma=False)
```

```python
import functools
import math

import jax
import jax.numpy as jnp
from jax import lax
from jax.experimental import pallas as pl
from jax.experimental.pallas import tpu as pltpu
from jax.sharding import PartitionSpec as P

DH = 128
LOW = -1e30
MESH = pl.DeviceIdType.MESH


def sides_of(axis, size):
    me = lax.axis_index(axis)
    if size == 1:
        return []
    if size == 2:
        return [(1 - me, None, 1)]
    return [(me - 1, me > 0, 2), (me + 1, me < size - 1, 1)]


def guarded(valid, fn):
    if valid is None:
        fn()
    else:
        pl.when(valid)(fn)


def flip(index, bits):
    step = 1
    while step <= bits:
        if bits // step % 2:
            index = index + step - 2 * step * (lax.rem(lax.div(index, step), 2))
        step *= 2
    return index


def kernel(
    sizes,
    rows,
    heads,
    q_ref,
    k_ref,
    v_ref,
    g_ref,
    o_ref,
    dq_ref,
    dk_ref,
    dv_ref,
    qg,
    win,
    s_ref,
    outb,
    own,
    r1s,
    r1r,
    r2s,
    r2r,
    in_s,
    in_r,
    px_s,
    px_r,
    py_s,
    py_r,
    hc_s,
    hc_r,
    bc_s,
    bc_r,
    bx_s,
    bx_r,
    by_s,
    by_r,
    ou_s,
    ou_r,
    lo_s,
):
    size_t, size_h, size_z = sizes
    tokens = rows * size_z
    z = lax.axis_index("head")
    ta = lax.axis_index("ta")
    corner = (ta == 0) | (ta == size_t - 1)
    inner = jnp.logical_not(corner)
    pair = flip(ta, 1)
    relay = size_t == 4
    across = flip(ta, 2) if relay else ta - 1 + 2 * lax.rem(ta, 2)
    sides = sides_of("ha", size_h)
    nt, nr = 3, 1 + len(sides)
    factor = 1.0 / math.sqrt(DH)
    scale = factor * math.log2(math.e)
    hops = list(range(size_z - 1, 0, -1))

    barrier = pltpu.get_barrier_semaphore()
    expected = size_z
    for d in hops:
        pl.semaphore_signal(barrier, inc=1, device_id={"head": flip(z, d)}, device_id_type=MESH)
    pl.semaphore_signal(barrier, inc=1, device_id={"ta": pair}, device_id_type=MESH)
    for axis, peer, valid in [("ta", across, None if relay else inner)] + [("ha", peer, valid) for peer, valid, _ in sides]:

        def greet(axis=axis, peer=peer):
            pl.semaphore_signal(barrier, inc=1, device_id={axis: peer}, device_id_type=MESH)

        guarded(valid, greet)
        expected = expected + (1 if valid is None else jnp.where(valid, 1, 0))
    pl.semaphore_wait(barrier, expected)

    def columns(group, h):
        return pl.ds(pl.multiple_of((group * heads + h) * DH, DH), DH)

    def part(group):
        return pl.ds(pl.multiple_of(group * rows, rows), rows)

    ins = (k_ref, v_ref, q_ref, g_ref)
    outs = (o_ref, dq_ref, dk_ref, dv_ref)

    def remote(src, dst, send, recv, device):
        return pltpu.make_async_remote_copy(
            src_ref=src, dst_ref=dst, send_sem=send, recv_sem=recv, device_id=device, device_id_type=MESH
        )

    def landing(h, a, group):
        if a < 2:
            return win.at[h, 0, 0, a, part(group), :]
        return qg.at[h, a - 2, part(group), :]

    def in_copy(h, a, d):
        peer = flip(z, d)
        return remote(ins[a].at[:, columns(peer, h)], landing(h, a, z), in_s.at[h, a, d], in_r.at[h, a, d], {"head": peer})

    def out_copy(h, a, d):
        peer = flip(z, d)
        return remote(outb.at[h, a, part(peer), :], outs[a].at[:, columns(z, h)], ou_s.at[h, a, d], ou_r.at[h, a, d], {"head": peer})

    def pair_copy(h, a):
        return remote(win.at[h, 0, 0, a], win.at[h, 0, 1, a], px_s.at[h, a], px_r.at[h, a], {"ta": pair})

    def across_copy(h, a):
        return remote(win.at[h, 0, 1 if relay else 0, a], win.at[h, 0, 2, a], py_s.at[h, a], py_r.at[h, a], {"ta": across})

    def side_copy(h, i, t):
        peer, _, there = sides[i]
        return remote(win.at[h, 0, t], win.at[h, there, t], hc_s.at[h, i, t], hc_r.at[h, there - 1, t], {"ha": peer})

    def back_side(h, i, t):
        peer, _, there = sides[i]
        return remote(r1s.at[h, i, t], r1r.at[h, there - 1, t], bc_s.at[h, i, t], bc_r.at[h, there - 1, t], {"ha": peer})

    def back_pair(h, a):
        return remote(r2s.at[h, 0, a], r2r.at[h, 0, a], bx_s.at[h, a], bx_r.at[h, a], {"ta": pair})

    def back_across(h, a):
        return remote(r2s.at[h, 1, a], r2r.at[h, 1, a], by_s.at[h, a], by_r.at[h, a], {"ta": across})

    def from_side(h, i, t):
        peer = sides[i][0]
        return remote(win.at[h, i + 1, t], win.at[h, i + 1, t], hc_r.at[h, i, t], hc_r.at[h, i, t], {"ha": peer})

    def back_from_side(h, i, t):
        peer = sides[i][0]
        return remote(r1r.at[h, i, t], r1r.at[h, i, t], bc_r.at[h, i, t], bc_r.at[h, i, t], {"ha": peer})

    def both(valid, other):
        return other if valid is None else valid & other

    def send_in(h, arrays):
        for a in arrays:
            for d in hops:
                in_copy(h, a, d).start()

    def send_kv(h):
        send_in(h, (0, 1))

    def send_qg(h):
        send_in(h, (2, 3))

    send_kv(0)
    if heads > 1:
        send_kv(1)
    send_qg(0)

    @pl.when(corner)
    def _():
        @pl.loop(0, heads)
        def _(h):
            for r in range(nr):
                win[h, r, 2] = jnp.zeros((2, tokens, DH), win.dtype)

    for i, (peer, valid, _) in enumerate(sides):
        if valid is not None:

            @pl.when(jnp.logical_not(valid))
            def _(i=i):
                @pl.loop(0, heads)
                def _(h):
                    win[h, i + 1] = jnp.zeros((nt, 2, tokens, DH), win.dtype)

    def local_copy(h, a):
        return pltpu.make_async_copy(ins[a].at[:, columns(z, h)], landing(h, a, z), lo_s.at[h, a])

    @pl.loop(0, heads)
    def _(h):
        for a in range(4):
            local_copy(h, a).start()

    def to_sides(h, t, cond=None):
        for i, (peer, valid, _) in enumerate(sides):
            go = valid if cond is None else both(valid, cond)
            guarded(go, lambda i=i: side_copy(h, i, t).start())

    def spread_own(h):
        for a in range(2):
            for d in hops:
                in_copy(h, a, d).wait_recv()
            local_copy(h, a).wait()
            pair_copy(h, a).start()
            if not relay:
                pl.when(inner)(lambda a=a: across_copy(h, a).start())
        to_sides(h, 0)

    def spread_pair(h):
        for a in range(2):
            pair_copy(h, a).wait_recv()
            if relay:
                pl.when(corner)(lambda a=a: across_copy(h, a).start())
        to_sides(h, 1)

    def spread_across(h):
        @pl.when(inner)
        def _():
            for a in range(2):
                across_copy(h, a).wait_recv()
            to_sides(h, 2)

    def score(h):
        for a in range(2, 4):
            for d in hops:
                in_copy(h, a, d).wait_recv()
            local_copy(h, a).wait()
        queries = qg[h, 0]
        highest = jnp.full((1, tokens), LOW, jnp.float32)
        for r in range(nr):
            for t in range(nt):
                if r > 0:
                    valid = sides[r - 1][1]
                    guarded(both(valid, inner) if t == 2 else valid, lambda r=r, t=t: from_side(h, r - 1, t).wait_recv())
                scores = lax.dot_general(win[h, r, t, 0], queries, (((1,), (1,)), ((), ())), preferred_element_type=jnp.float32) * scale
                for cond in ([inner] if t == 2 else []) + ([sides[r - 1][1]] if r > 0 else []):
                    if cond is not None:
                        scores = jnp.where(cond, scores, LOW)
                s_ref[r * nt + t] = scores
                highest = jnp.maximum(highest, jnp.max(scores, axis=0, keepdims=True))
        return highest

    def forward(h, highest):
        grads = qg[h, 1]
        total = jnp.zeros((1, tokens), jnp.float32)
        mixed = jnp.zeros((DH, tokens), jnp.float32)
        for r in range(nr):
            for t in range(nt):
                weights = jnp.exp2(s_ref[r * nt + t] - highest)
                s_ref[r * nt + t] = weights
                total = total + jnp.sum(weights, axis=0, keepdims=True)
                mixed = mixed + lax.dot_general(
                    win[h, r, t, 1], weights.astype(jnp.bfloat16), (((0,), (0,)), ((), ())), preferred_element_type=jnp.float32
                )
        inverse = 1.0 / total
        attended = jnp.transpose(mixed * inverse).astype(jnp.bfloat16)
        outb[h, 0] = attended
        products = grads.astype(jnp.float32) * attended.astype(jnp.float32)
        row_dot = jnp.sum(jnp.transpose(products), axis=0, keepdims=True)
        for d in hops:
            out_copy(h, 0, d).start()
        return inverse, row_dot

    def backward(h, inverse, row_dot, query_grad, rs):
        queries = qg[h, 0]
        grads = qg[h, 1]
        for r in rs:
            for t in reversed(range(nt)):
                keys, values = win[h, r, t, 0], win[h, r, t, 1]
                probs = s_ref[r * nt + t] * inverse
                value_term = jnp.dot(probs.astype(jnp.bfloat16), grads, preferred_element_type=jnp.float32)
                prob_grad = lax.dot_general(values, grads, (((1,), (1,)), ((), ())), preferred_element_type=jnp.float32)
                score_grad = (probs * (prob_grad - row_dot)).astype(jnp.bfloat16)
                query_grad = query_grad + lax.dot_general(
                    keys, score_grad, (((0,), (0,)), ((), ())), preferred_element_type=jnp.float32
                )
                key_term = jnp.dot(score_grad, queries, preferred_element_type=jnp.float32) * factor
                if r == 0:
                    own[h, t, 0] = key_term
                    own[h, t, 1] = value_term
                else:
                    r1s[h, r - 1, t, 0] = key_term.astype(jnp.bfloat16)
                    r1s[h, r - 1, t, 1] = value_term.astype(jnp.bfloat16)
                    valid = sides[r - 1][1]
                    guarded(both(valid, inner) if t == 2 else valid, lambda r=r, t=t: back_side(h, r - 1, t).start())
        return query_grad

    def send_query_grad(h, query_grad):
        outb[h, 1] = jnp.transpose(query_grad * factor).astype(jnp.bfloat16)
        for d in hops:
            out_copy(h, 1, d).start()

    def fold_sides(h):
        for t in reversed(range(nt)):
            for i, (peer, valid, _) in enumerate(sides):

                def fold(i=i, t=t):
                    back_from_side(h, i, t).wait_recv()
                    own[h, t] = own[h, t] + r1r[h, i, t].astype(jnp.float32)

                guarded(both(valid, inner) if t == 2 else valid, fold)
            if t > 0:

                def send(t=t):
                    for a in range(2):
                        r2s[h, t - 1, a] = own[h, t, a].astype(jnp.bfloat16)
                        (back_across if t == 2 else back_pair)(h, a).start()

                guarded(inner if relay or t == 2 else None, send)

    def fold_across(h):
        @pl.when(corner if relay else inner)
        def _():
            for a in range(2):
                back_across(h, a).wait_recv()
                if relay:
                    r2s[h, 0, a] = (own[h, 1, a] + r2r[h, 1, a].astype(jnp.float32)).astype(jnp.bfloat16)
                    back_pair(h, a).start()
                else:
                    own[h, 0, a] = own[h, 0, a] + r2r[h, 1, a].astype(jnp.float32)

    def fold_pair(h):
        for a in range(2):
            back_pair(h, a).wait_recv()
            outb[h, a + 2] = (own[h, 0, a] + r2r[h, 0, a].astype(jnp.float32)).astype(jnp.bfloat16)
            for d in hops:
                out_copy(h, a + 2, d).start()
        for a in range(4):
            outs[a][:, columns(z, h)] = outb[h, a, part(z), :]

    def later(h, fn):
        pl.when(h < heads)(lambda: fn(h))

    def earlier(h, fn):
        pl.when(h >= 0)(lambda: fn(h))

    spread_own(0)
    if heads > 2:
        send_kv(2)
    if heads > 1:
        spread_own(1)
        send_qg(1)
    spread_pair(0)
    spread_across(0)

    @pl.loop(0, heads)
    def _(h):
        highest = score(h)
        later(h + 3, send_kv)
        later(h + 1, spread_pair)
        inverse, row_dot = forward(h, highest)
        later(h + 1, spread_across)
        earlier(h - 1, fold_across)
        later(h + 2, spread_own)
        later(h + 2, send_qg)
        query_grad = backward(h, inverse, row_dot, jnp.zeros((DH, tokens), jnp.float32), range(nr - 1, -1, -1))
        send_query_grad(h, query_grad)
        fold_sides(h)
        earlier(h - 1, fold_pair)

    fold_across(heads - 1)
    fold_pair(heads - 1)

    @pl.loop(0, heads)
    def _(h):
        for a in range(4):
            for d in hops:
                in_copy(h, a, d).wait_send()
                out_copy(h, a, d).wait_recv()
                out_copy(h, a, d).wait_send()
        for a in range(2):
            pair_copy(h, a).wait_send()
            back_pair(h, a).wait_send()
            pl.when(corner if relay else inner)(lambda a=a: across_copy(h, a).wait_send())
            pl.when(inner)(lambda a=a: back_across(h, a).wait_send())
        for i, (peer, valid, _) in enumerate(sides):
            for t in range(nt):

                def drain(i=i, t=t):
                    side_copy(h, i, t).wait_send()
                    back_side(h, i, t).wait_send()

                guarded(both(valid, inner) if t == 2 else valid, drain)


def store(*refs):
    sems = refs[8]
    copies = [pltpu.make_async_copy(refs[i], refs[4 + i], sems.at[i]) for i in range(4)]
    for copy in copies:
        copy.start()
    for copy in copies:
        copy.wait()


def body(queries, keys, values, out_grad):
    sizes = tuple(lax.axis_size(axis) for axis in ("ta", "ha", "head"))
    size_t, size_h, size_z = sizes
    assert size_t % 2 == 0 and size_z & (size_z - 1) == 0
    shape = queries.shape
    rows = shape[0] * shape[1] * shape[2]
    width = shape[3]
    heads = width // DH // size_z
    tokens = rows * size_z
    nt, nr = 3, min(3, size_h)
    bf16 = jnp.bfloat16
    dma = pltpu.SemaphoreType.DMA
    mr = max(1, nr - 1)
    flat = [x.reshape(rows, width) for x in (queries, keys, values, out_grad)]
    outs = pl.pallas_call(
        functools.partial(kernel, sizes, rows, heads),
        out_shape=[pltpu.VMEM((rows, width), bf16)] * 4,
        in_specs=[pl.BlockSpec(memory_space=pl.ANY)] * 4,
        out_specs=[pl.BlockSpec(memory_space=pltpu.VMEM)] * 4,
        scratch_shapes=[
            pltpu.VMEM((heads, 2, tokens, DH), bf16),
            pltpu.VMEM((heads, nr, nt, 2, tokens, DH), bf16),
            pltpu.VMEM((nr * nt, tokens, tokens), jnp.float32),
            pltpu.VMEM((heads, 4, tokens, DH), bf16),
            pltpu.VMEM((heads, nt, 2, tokens, DH), jnp.float32),
            pltpu.VMEM((heads, mr, nt, 2, tokens, DH), bf16),
            pltpu.VMEM((heads, mr, nt, 2, tokens, DH), bf16),
            pltpu.VMEM((heads, 2, 2, tokens, DH), bf16),
            pltpu.VMEM((heads, 2, 2, tokens, DH), bf16),
            dma((heads, 4, size_z)),
            dma((heads, 4, size_z)),
            dma((heads, 2)),
            dma((heads, 2)),
            dma((heads, 2)),
            dma((heads, 2)),
            dma((heads, mr, nt)),
            dma((heads, mr, nt)),
            dma((heads, mr, nt)),
            dma((heads, mr, nt)),
            dma((heads, 2)),
            dma((heads, 2)),
            dma((heads, 2)),
            dma((heads, 2)),
            dma((heads, 4, size_z)),
            dma((heads, 4, size_z)),
            dma((heads, 4)),
        ],
        compiler_params=pltpu.CompilerParams(collective_id=0, has_side_effects=True, vmem_limit_bytes=56 * 1024 * 1024),
        name="tile_attention",
    )(*flat)
    outs = [pltpu.with_memory_space_constraint(x, pltpu.VMEM) for x in outs]
    outs = pl.pallas_call(
        store,
        out_shape=[jax.ShapeDtypeStruct((rows, width), bf16)] * 4,
        in_specs=[pl.BlockSpec(memory_space=pl.ANY)] * 4,
        out_specs=[pl.BlockSpec(memory_space=pl.ANY)] * 4,
        scratch_shapes=[dma((4,))],
        name="store",
    )(*outs)
    return tuple(x.reshape(shape) for x in outs)


def solution(mesh):
    spec = P("ta", ("ha", "head"), None, None)
    return jax.shard_map(body, mesh=mesh, in_specs=(spec,) * 4, out_specs=(spec,) * 4, check_vma=False)
```

```python
import functools
import math

import jax
import jax.numpy as jnp
from jax import lax
from jax.experimental import pallas as pl
from jax.experimental.pallas import tpu as pltpu
from jax.sharding import PartitionSpec as P

DH = 128
LOW = -1e30
MESH = pl.DeviceIdType.MESH


def sides_of(axis, size):
    me = lax.axis_index(axis)
    if size == 1:
        return []
    if size == 2:
        return [(1 - me, None, 1)]
    return [(me - 1, me > 0, 2), (me + 1, me < size - 1, 1)]


def guarded(valid, fn):
    if valid is None:
        fn()
    else:
        pl.when(valid)(fn)


def flip(index, bits):
    step = 1
    while step <= bits:
        if bits // step % 2:
            index = index + step - 2 * step * (lax.rem(lax.div(index, step), 2))
        step *= 2
    return index


def differ(one, other, size):
    bits, step = 0, 1
    while step < size:
        bits = bits + step * lax.rem(lax.div(one, step) + lax.div(other, step), 2)
        step *= 2
    return bits


def kernel(
    sizes,
    rows,
    heads,
    q_ref,
    k_ref,
    v_ref,
    g_ref,
    out_ref,
    qg,
    win,
    stage,
    s_ref,
    outb,
    own,
    r1s,
    r1r,
    r2s,
    r2r,
    in_s,
    in_r,
    px_s,
    px_r,
    py_s,
    py_r,
    hc_s,
    hc_r,
    bc_s,
    bc_r,
    bx_s,
    bx_r,
    by_s,
    by_r,
    ou_s,
    ou_r,
    lo_s,
    st_s,
):
    size_t, size_h, size_z = sizes
    tokens = rows * size_z
    z = lax.axis_index("head")
    ta = lax.axis_index("ta")
    corner = (ta == 0) | (ta == size_t - 1)
    inner = jnp.logical_not(corner)
    pair = flip(ta, 1)
    relay = size_t == 4
    across = flip(ta, 2) if relay else ta - 1 + 2 * lax.rem(ta, 2)
    sides = sides_of("ha", size_h)
    nt, nr = 3, 1 + len(sides)
    factor = 1.0 / math.sqrt(DH)
    scale = factor * math.log2(math.e)
    hops = list(range(size_z - 1, 0, -1))

    barrier = pltpu.get_barrier_semaphore()
    expected = size_z
    for d in hops:
        pl.semaphore_signal(barrier, inc=1, device_id={"head": flip(z, d)}, device_id_type=MESH)
    pl.semaphore_signal(barrier, inc=1, device_id={"ta": pair}, device_id_type=MESH)
    for axis, peer, valid in [("ta", across, None if relay else inner)] + [("ha", peer, valid) for peer, valid, _ in sides]:

        def greet(axis=axis, peer=peer):
            pl.semaphore_signal(barrier, inc=1, device_id={axis: peer}, device_id_type=MESH)

        guarded(valid, greet)
        expected = expected + (1 if valid is None else jnp.where(valid, 1, 0))
    def columns(group, h):
        return pl.ds(pl.multiple_of((group * heads + h) * DH, DH), DH)

    def part(group):
        return pl.ds(pl.multiple_of(group * rows, rows), rows)

    ins = (k_ref, v_ref, q_ref, g_ref)

    def remote(src, dst, send, recv, device):
        return pltpu.make_async_remote_copy(
            src_ref=src, dst_ref=dst, send_sem=send, recv_sem=recv, device_id=device, device_id_type=MESH
        )

    def landing(h, p):
        return win.at[h, 0, 0, :, part(z), :] if p == 0 else qg.at[h, :, part(z), :]

    def stage_copy(h, a, d):
        return pltpu.make_async_copy(ins[a].at[:, columns(flip(z, d), h)], stage.at[h, a // 2, d - 1, a % 2], st_s.at[h, a, d])

    def local_copy(h, a):
        return pltpu.make_async_copy(ins[a].at[:, columns(z, h)], landing(h, a // 2).at[a % 2], lo_s.at[h, a])

    def in_copy(h, p, d):
        return remote(stage.at[h, p, d - 1], landing(h, p), in_s.at[h, p, d], in_r.at[h, p, d], {"head": flip(z, d)})

    def out_copy(h, p, d, peer=None):
        peer = flip(z, d) if peer is None else peer
        return remote(
            outb.at[h, pl.ds(2 * p, 2), part(peer), :],
            out_ref.at[pl.ds(2 * p, 2), :, columns(z, h)],
            ou_s.at[h, p, d],
            ou_r.at[h, p, d],
            {"head": peer},
        )

    def pair_copy(h, a):
        return remote(win.at[h, 0, 0, a], win.at[h, 0, 1, a], px_s.at[h, a], px_r.at[h, a], {"ta": pair})

    def across_copy(h, a):
        return remote(win.at[h, 0, 1 if relay else 0, a], win.at[h, 0, 2, a], py_s.at[h, a], py_r.at[h, a], {"ta": across})

    def side_copy(h, i, t):
        peer, _, there = sides[i]
        return remote(win.at[h, 0, t], win.at[h, there, t], hc_s.at[h, i, t], hc_r.at[h, there - 1, t], {"ha": peer})

    def back_side(h, i, t):
        peer, _, there = sides[i]
        return remote(r1s.at[h, i, t], r1r.at[h, there - 1, t], bc_s.at[h, i, t], bc_r.at[h, there - 1, t], {"ha": peer})

    def back_pair(h, a):
        return remote(r2s.at[h, 0, a], r2r.at[h, 0, a], bx_s.at[h, a], bx_r.at[h, a], {"ta": pair})

    def back_across(h, a):
        return remote(r2s.at[h, 1, a], r2r.at[h, 1, a], by_s.at[h, a], by_r.at[h, a], {"ta": across})

    def from_side(h, i, t):
        peer = sides[i][0]
        return remote(win.at[h, i + 1, t], win.at[h, i + 1, t], hc_r.at[h, i, t], hc_r.at[h, i, t], {"ha": peer})

    def back_from_side(h, i, t):
        peer = sides[i][0]
        return remote(r1r.at[h, i, t], r1r.at[h, i, t], bc_r.at[h, i, t], bc_r.at[h, i, t], {"ha": peer})

    def both(valid, other):
        return other if valid is None else valid & other

    def send_in(h, p):
        for d in hops:
            for a in (2 * p, 2 * p + 1):
                stage_copy(h, a, d).wait()
            in_copy(h, p, d).start()

    def send_kv(h):
        send_in(h, 0)

    def send_qg(h):
        send_in(h, 1)

    def send_out(h, p):
        for i in range(size_z - 1):
            peer = jnp.where(z == 0, size_z - 1 - i, jnp.where(i >= z, i + 1, i))
            out_copy(h, p, differ(z, peer, size_z), peer).start()

    for p in range(2):
        for h in range(heads):
            for a in (2 * p, 2 * p + 1):
                for d in hops:
                    stage_copy(h, a, d).start()
                local_copy(h, a).start()
    pl.semaphore_wait(barrier, expected)

    send_kv(0)
    if heads > 1:
        send_kv(1)
    send_qg(0)

    @pl.when(corner)
    def _():
        @pl.loop(0, heads)
        def _(h):
            for r in range(nr):
                win[h, r, 2] = jnp.zeros((2, tokens, DH), win.dtype)

    for i, (peer, valid, _) in enumerate(sides):
        if valid is not None:

            @pl.when(jnp.logical_not(valid))
            def _(i=i):
                @pl.loop(0, heads)
                def _(h):
                    win[h, i + 1] = jnp.zeros((nt, 2, tokens, DH), win.dtype)


    def to_sides(h, t, cond=None):
        for i, (peer, valid, _) in enumerate(sides):
            go = valid if cond is None else both(valid, cond)
            guarded(go, lambda i=i: side_copy(h, i, t).start())

    def spread_own(h):
        for d in hops:
            in_copy(h, 0, d).wait_recv()
        for a in range(2):
            local_copy(h, a).wait()
            pair_copy(h, a).start()
            if not relay:
                pl.when(inner)(lambda a=a: across_copy(h, a).start())
        to_sides(h, 0)

    def spread_pair(h):
        for a in range(2):
            pair_copy(h, a).wait_recv()
            if relay:
                pl.when(corner)(lambda a=a: across_copy(h, a).start())
        to_sides(h, 1)

    def spread_across(h):
        @pl.when(inner)
        def _():
            for a in range(2):
                across_copy(h, a).wait_recv()
            to_sides(h, 2)

    def score(h):
        for d in hops:
            in_copy(h, 1, d).wait_recv()
        for a in range(2, 4):
            local_copy(h, a).wait()
        queries = qg[h, 0]
        highest = jnp.full((1, tokens), LOW, jnp.float32)
        for r in range(nr):
            for t in range(nt):
                if r > 0:
                    valid = sides[r - 1][1]
                    guarded(both(valid, inner) if t == 2 else valid, lambda r=r, t=t: from_side(h, r - 1, t).wait_recv())
                scores = lax.dot_general(win[h, r, t, 0], queries, (((1,), (1,)), ((), ())), preferred_element_type=jnp.float32) * scale
                for cond in ([inner] if t == 2 else []) + ([sides[r - 1][1]] if r > 0 else []):
                    if cond is not None:
                        scores = jnp.where(cond, scores, LOW)
                s_ref[r * nt + t] = scores
                highest = jnp.maximum(highest, jnp.max(scores, axis=0, keepdims=True))
        return highest

    def forward(h, highest):
        grads = qg[h, 1]
        total = jnp.zeros((1, tokens), jnp.float32)
        mixed = jnp.zeros((DH, tokens), jnp.float32)
        for r in range(nr):
            for t in range(nt):
                weights = jnp.exp2(s_ref[r * nt + t] - highest)
                s_ref[r * nt + t] = weights
                total = total + jnp.sum(weights, axis=0, keepdims=True)
                mixed = mixed + lax.dot_general(
                    win[h, r, t, 1], weights.astype(jnp.bfloat16), (((0,), (0,)), ((), ())), preferred_element_type=jnp.float32
                )
        inverse = 1.0 / total
        attended = jnp.transpose(mixed * inverse).astype(jnp.bfloat16)
        outb[h, 0] = attended
        products = grads.astype(jnp.float32) * attended.astype(jnp.float32)
        row_dot = jnp.sum(jnp.transpose(products), axis=0, keepdims=True)
        return inverse, row_dot

    def backward(h, inverse, row_dot, query_grad, rs):
        queries = qg[h, 0]
        grads = qg[h, 1]
        for r in rs:
            for t in reversed(range(nt)):
                keys, values = win[h, r, t, 0], win[h, r, t, 1]
                probs = s_ref[r * nt + t] * inverse
                value_term = jnp.dot(probs.astype(jnp.bfloat16), grads, preferred_element_type=jnp.float32)
                prob_grad = lax.dot_general(values, grads, (((1,), (1,)), ((), ())), preferred_element_type=jnp.float32)
                score_grad = (probs * (prob_grad - row_dot)).astype(jnp.bfloat16)
                query_grad = query_grad + lax.dot_general(
                    keys, score_grad, (((0,), (0,)), ((), ())), preferred_element_type=jnp.float32
                )
                key_term = jnp.dot(score_grad, queries, preferred_element_type=jnp.float32) * factor
                if r == 0:
                    own[h, t, 0] = key_term
                    own[h, t, 1] = value_term
                else:
                    r1s[h, r - 1, t, 0] = key_term.astype(jnp.bfloat16)
                    r1s[h, r - 1, t, 1] = value_term.astype(jnp.bfloat16)
                    valid = sides[r - 1][1]
                    guarded(both(valid, inner) if t == 2 else valid, lambda r=r, t=t: back_side(h, r - 1, t).start())
        return query_grad

    def send_query_grad(h, query_grad):
        outb[h, 1] = jnp.transpose(query_grad * factor).astype(jnp.bfloat16)
        send_out(h, 0)

    def fold_sides(h):
        for t in reversed(range(nt)):
            for i, (peer, valid, _) in enumerate(sides):

                def fold(i=i, t=t):
                    back_from_side(h, i, t).wait_recv()
                    own[h, t] = own[h, t] + r1r[h, i, t].astype(jnp.float32)

                guarded(both(valid, inner) if t == 2 else valid, fold)
            if t > 0:

                def send(t=t):
                    for a in range(2):
                        r2s[h, t - 1, a] = own[h, t, a].astype(jnp.bfloat16)
                        (back_across if t == 2 else back_pair)(h, a).start()

                guarded(inner if relay or t == 2 else None, send)

    def fold_across(h):
        @pl.when(corner if relay else inner)
        def _():
            for a in range(2):
                back_across(h, a).wait_recv()
                if relay:
                    r2s[h, 0, a] = (own[h, 1, a] + r2r[h, 1, a].astype(jnp.float32)).astype(jnp.bfloat16)
                    back_pair(h, a).start()
                else:
                    own[h, 0, a] = own[h, 0, a] + r2r[h, 1, a].astype(jnp.float32)

    def fold_pair(h):
        for a in range(2):
            back_pair(h, a).wait_recv()
            outb[h, a + 2] = (own[h, 0, a] + r2r[h, 0, a].astype(jnp.float32)).astype(jnp.bfloat16)
        send_out(h, 1)
        for a in range(4):
            out_ref[a, :, columns(z, h)] = outb[h, a, part(z), :]

    def later(h, fn):
        pl.when(h < heads)(lambda: fn(h))

    def earlier(h, fn):
        pl.when(h >= 0)(lambda: fn(h))

    spread_own(0)
    if heads > 2:
        send_kv(2)
    if heads > 1:
        spread_own(1)
        send_qg(1)
    spread_pair(0)
    spread_across(0)

    @pl.loop(0, heads)
    def _(h):
        highest = score(h)
        later(h + 3, send_kv)
        later(h + 1, spread_pair)
        inverse, row_dot = forward(h, highest)
        earlier(h - 2, fold_pair)
        later(h + 2, spread_own)
        later(h + 2, send_qg)
        query_grad = backward(h, inverse, row_dot, jnp.zeros((DH, tokens), jnp.float32), range(nr - 1, 0, -1))
        earlier(h - 1, fold_across)
        query_grad = backward(h, inverse, row_dot, query_grad, (0,))
        send_query_grad(h, query_grad)
        fold_sides(h)
        later(h + 1, spread_across)

    if heads > 1:
        fold_pair(heads - 2)
    fold_across(heads - 1)
    fold_pair(heads - 1)

    @pl.loop(0, heads)
    def _(h):
        for p in range(2):
            for d in hops:
                in_copy(h, p, d).wait_send()
                out_copy(h, p, d).wait_recv()
                out_copy(h, p, d).wait_send()
        for a in range(2):
            pair_copy(h, a).wait_send()
            back_pair(h, a).wait_send()
            pl.when(corner if relay else inner)(lambda a=a: across_copy(h, a).wait_send())
            pl.when(inner)(lambda a=a: back_across(h, a).wait_send())
        for i, (peer, valid, _) in enumerate(sides):
            for t in range(nt):

                def drain(i=i, t=t):
                    side_copy(h, i, t).wait_send()
                    back_side(h, i, t).wait_send()

                guarded(both(valid, inner) if t == 2 else valid, drain)


def store(held, *refs):
    sems = refs[4]
    copies = [pltpu.make_async_copy(held.at[i], refs[i], sems.at[i]) for i in range(4)]
    for copy in copies:
        copy.start()
    for copy in copies:
        copy.wait()


def body(queries, keys, values, out_grad):
    sizes = tuple(lax.axis_size(axis) for axis in ("ta", "ha", "head"))
    size_t, size_h, size_z = sizes
    assert size_t % 2 == 0 and size_z & (size_z - 1) == 0
    shape = queries.shape
    rows = shape[0] * shape[1] * shape[2]
    width = shape[3]
    heads = width // DH // size_z
    tokens = rows * size_z
    nt, nr = 3, min(3, size_h)
    bf16 = jnp.bfloat16
    dma = pltpu.SemaphoreType.DMA
    mr = max(1, nr - 1)
    flat = [x.reshape(rows, width) for x in (queries, keys, values, out_grad)]
    held = pl.pallas_call(
        functools.partial(kernel, sizes, rows, heads),
        out_shape=pltpu.VMEM((4, rows, width), bf16),
        in_specs=[pl.BlockSpec(memory_space=pl.ANY)] * 4,
        out_specs=pl.BlockSpec(memory_space=pltpu.VMEM),
        scratch_shapes=[
            pltpu.VMEM((heads, 2, tokens, DH), bf16),
            pltpu.VMEM((heads, nr, nt, 2, tokens, DH), bf16),
            pltpu.VMEM((heads, 2, size_z - 1, 2, rows, DH), bf16),
            pltpu.VMEM((nr * nt, tokens, tokens), jnp.float32),
            pltpu.VMEM((heads, 4, tokens, DH), bf16),
            pltpu.VMEM((heads, nt, 2, tokens, DH), jnp.float32),
            pltpu.VMEM((heads, mr, nt, 2, tokens, DH), bf16),
            pltpu.VMEM((heads, mr, nt, 2, tokens, DH), bf16),
            pltpu.VMEM((heads, 2, 2, tokens, DH), bf16),
            pltpu.VMEM((heads, 2, 2, tokens, DH), bf16),
            dma((heads, 2, size_z)),
            dma((heads, 2, size_z)),
            dma((heads, 2)),
            dma((heads, 2)),
            dma((heads, 2)),
            dma((heads, 2)),
            dma((heads, mr, nt)),
            dma((heads, mr, nt)),
            dma((heads, mr, nt)),
            dma((heads, mr, nt)),
            dma((heads, 2)),
            dma((heads, 2)),
            dma((heads, 2)),
            dma((heads, 2)),
            dma((heads, 2, size_z)),
            dma((heads, 2, size_z)),
            dma((heads, 4)),
            dma((heads, 4, size_z)),
        ],
        compiler_params=pltpu.CompilerParams(collective_id=0, has_side_effects=True, vmem_limit_bytes=56 * 1024 * 1024),
        name="tile_attention",
    )(*flat)
    outs = pl.pallas_call(
        store,
        out_shape=[jax.ShapeDtypeStruct((rows, width), bf16)] * 4,
        in_specs=[pl.BlockSpec(memory_space=pl.ANY)],
        out_specs=[pl.BlockSpec(memory_space=pl.ANY)] * 4,
        scratch_shapes=[dma((4,))],
        name="store",
    )(pltpu.with_memory_space_constraint(held, pltpu.VMEM))
    return tuple(x.reshape(shape) for x in outs)


def solution(mesh):
    spec = P("ta", ("ha", "head"), None, None)
    return jax.shard_map(body, mesh=mesh, in_specs=(spec,) * 4, out_specs=(spec,) * 4, check_vma=False)
```

```python
import functools
import math

import jax
import jax.numpy as jnp
from jax import lax
from jax.experimental import pallas as pl
from jax.experimental.pallas import tpu as pltpu
from jax.sharding import PartitionSpec as P

DH = 128
LOW = -1e30
MESH = pl.DeviceIdType.MESH


def sides_of(axis, size):
    me = lax.axis_index(axis)
    if size == 1:
        return []
    if size == 2:
        return [(1 - me, None, 1)]
    return [(me - 1, me > 0, 2), (me + 1, me < size - 1, 1)]


def guarded(valid, fn):
    if valid is None:
        fn()
    else:
        pl.when(valid)(fn)


def flip(index, bits):
    step = 1
    while step <= bits:
        if bits // step % 2:
            index = index + step - 2 * step * (lax.rem(lax.div(index, step), 2))
        step *= 2
    return index


def differ(one, other, size):
    bits, step = 0, 1
    while step < size:
        bits = bits + step * lax.rem(lax.div(one, step) + lax.div(other, step), 2)
        step *= 2
    return bits


def kernel(
    sizes,
    rows,
    heads,
    q_ref,
    k_ref,
    v_ref,
    g_ref,
    out_ref,
    qg,
    win,
    stage,
    s_ref,
    outb,
    own,
    r1s,
    r1r,
    r2s,
    r2r,
    in_s,
    in_r,
    px_s,
    px_r,
    py_s,
    py_r,
    hc_s,
    hc_r,
    bc_s,
    bc_r,
    bx_s,
    bx_r,
    by_s,
    by_r,
    ou_s,
    ou_r,
    lo_s,
    st_s,
):
    size_t, size_h, size_z = sizes
    tokens = rows * size_z
    z = lax.axis_index("head")
    ta = lax.axis_index("ta")
    corner = (ta == 0) | (ta == size_t - 1)
    inner = jnp.logical_not(corner)
    pair = flip(ta, 1)
    relay = size_t == 4
    across = flip(ta, 2) if relay else ta - 1 + 2 * lax.rem(ta, 2)
    sides = sides_of("ha", size_h)
    nt, nr = 3, 1 + len(sides)
    factor = 1.0 / math.sqrt(DH)
    scale = factor * math.log2(math.e)
    hops = list(range(size_z - 1, 0, -1))

    barrier = pltpu.get_barrier_semaphore()
    expected = size_z
    for d in hops:
        pl.semaphore_signal(barrier, inc=1, device_id={"head": flip(z, d)}, device_id_type=MESH)
    pl.semaphore_signal(barrier, inc=1, device_id={"ta": pair}, device_id_type=MESH)
    for axis, peer, valid in [("ta", across, None if relay else inner)] + [("ha", peer, valid) for peer, valid, _ in sides]:

        def greet(axis=axis, peer=peer):
            pl.semaphore_signal(barrier, inc=1, device_id={axis: peer}, device_id_type=MESH)

        guarded(valid, greet)
        expected = expected + (1 if valid is None else jnp.where(valid, 1, 0))
    def columns(group, h):
        return pl.ds(pl.multiple_of((group * heads + h) * DH, DH), DH)

    def part(group):
        return pl.ds(pl.multiple_of(group * rows, rows), rows)

    ins = (k_ref, v_ref, q_ref, g_ref)

    def remote(src, dst, send, recv, device):
        return pltpu.make_async_remote_copy(
            src_ref=src, dst_ref=dst, send_sem=send, recv_sem=recv, device_id=device, device_id_type=MESH
        )

    def landing(h, p):
        return win.at[h, 0, 0, :, part(z), :] if p == 0 else qg.at[h, :, part(z), :]

    def stage_copy(h, a, d):
        return pltpu.make_async_copy(ins[a].at[:, columns(flip(z, d), h)], stage.at[h, a // 2, d - 1, a % 2], st_s.at[h, a, d])

    def local_copy(h, a):
        return pltpu.make_async_copy(ins[a].at[:, columns(z, h)], landing(h, a // 2).at[a % 2], lo_s.at[h, a])

    def in_copy(h, p, d):
        return remote(stage.at[h, p, d - 1], landing(h, p), in_s.at[h, p, d], in_r.at[h, p, d], {"head": flip(z, d)})

    def out_copy(h, p, d, peer=None):
        peer = flip(z, d) if peer is None else peer
        return remote(
            outb.at[h, pl.ds(2 * p, 2), part(peer), :],
            out_ref.at[pl.ds(2 * p, 2), :, columns(z, h)],
            ou_s.at[h, p, d],
            ou_r.at[h, p, d],
            {"head": peer},
        )

    def pair_copy(h, a):
        return remote(win.at[h, 0, 0, a], win.at[h, 0, 1, a], px_s.at[h, a], px_r.at[h, a], {"ta": pair})

    def across_copy(h, a):
        return remote(win.at[h, 0, 1 if relay else 0, a], win.at[h, 0, 2, a], py_s.at[h, a], py_r.at[h, a], {"ta": across})

    def side_copy(h, i, t):
        peer, _, there = sides[i]
        return remote(win.at[h, 0, t], win.at[h, there, t], hc_s.at[h, i, t], hc_r.at[h, there - 1, t], {"ha": peer})

    def back_side(h, i, t):
        peer, _, there = sides[i]
        return remote(r1s.at[h, i, t], r1r.at[h, there - 1, t], bc_s.at[h, i, t], bc_r.at[h, there - 1, t], {"ha": peer})

    def back_pair(h, a):
        return remote(r2s.at[h, 0, a], r2r.at[h, 0, a], bx_s.at[h, a], bx_r.at[h, a], {"ta": pair})

    def back_across(h, a):
        return remote(r2s.at[h, 1, a], r2r.at[h, 1, a], by_s.at[h, a], by_r.at[h, a], {"ta": across})

    def from_side(h, i, t):
        peer = sides[i][0]
        return remote(win.at[h, i + 1, t], win.at[h, i + 1, t], hc_r.at[h, i, t], hc_r.at[h, i, t], {"ha": peer})

    def back_from_side(h, i, t):
        peer = sides[i][0]
        return remote(r1r.at[h, i, t], r1r.at[h, i, t], bc_r.at[h, i, t], bc_r.at[h, i, t], {"ha": peer})

    def both(valid, other):
        return other if valid is None else valid & other

    def send_in(h, p):
        for d in hops:
            for a in (2 * p, 2 * p + 1):
                stage_copy(h, a, d).wait()
            in_copy(h, p, d).start()

    def send_kv(h):
        send_in(h, 0)

    def send_qg(h):
        send_in(h, 1)

    def send_step(h, p, i):
        peer = jnp.where(z == 0, size_z - 1 - i, jnp.where(i >= z, i + 1, i))
        out_copy(h, p, differ(z, peer, size_z), peer).start()

    def send_out(h, p):
        for i in range(size_z - 1):
            send_step(h, p, i)

    def send_ahead(h, p):
        send_step(h, p, 0)

        @pl.when(z == 0)
        def _():
            for i in range(1, size_z - 1):
                send_step(h, p, i)

    def send_rest(h, p):
        @pl.when(z != 0)
        def _():
            for i in range(1, size_z - 1):
                send_step(h, p, i)

    for p in range(2):
        for h in range(heads):
            for a in (2 * p, 2 * p + 1):
                for d in hops:
                    stage_copy(h, a, d).start()
                local_copy(h, a).start()
    pl.semaphore_wait(barrier, expected)

    send_kv(0)
    if heads > 1:
        send_kv(1)
    send_qg(0)

    @pl.when(corner)
    def _():
        @pl.loop(0, heads)
        def _(h):
            for r in range(nr):
                win[h, r, 2] = jnp.zeros((2, tokens, DH), win.dtype)

    for i, (peer, valid, _) in enumerate(sides):
        if valid is not None:

            @pl.when(jnp.logical_not(valid))
            def _(i=i):
                @pl.loop(0, heads)
                def _(h):
                    win[h, i + 1] = jnp.zeros((nt, 2, tokens, DH), win.dtype)


    def to_sides(h, t, cond=None):
        for i, (peer, valid, _) in enumerate(sides):
            go = valid if cond is None else both(valid, cond)
            guarded(go, lambda i=i: side_copy(h, i, t).start())

    def spread_own(h):
        for d in hops:
            in_copy(h, 0, d).wait_recv()
        for a in range(2):
            local_copy(h, a).wait()
            pair_copy(h, a).start()
            if not relay:
                pl.when(inner)(lambda a=a: across_copy(h, a).start())
        to_sides(h, 0)

    def spread_pair(h):
        for a in range(2):
            pair_copy(h, a).wait_recv()
            if relay:
                pl.when(corner)(lambda a=a: across_copy(h, a).start())
        to_sides(h, 1)

    def spread_across(h):
        @pl.when(inner)
        def _():
            for a in range(2):
                across_copy(h, a).wait_recv()
            to_sides(h, 2)

    def score(h):
        for d in hops:
            in_copy(h, 1, d).wait_recv()
        for a in range(2, 4):
            local_copy(h, a).wait()
        queries = qg[h, 0]
        highest = jnp.full((1, tokens), LOW, jnp.float32)
        for r in range(nr):
            for t in range(nt):
                if r > 0:
                    valid = sides[r - 1][1]
                    guarded(both(valid, inner) if t == 2 else valid, lambda r=r, t=t: from_side(h, r - 1, t).wait_recv())
                scores = lax.dot_general(win[h, r, t, 0], queries, (((1,), (1,)), ((), ())), preferred_element_type=jnp.float32) * scale
                for cond in ([inner] if t == 2 else []) + ([sides[r - 1][1]] if r > 0 else []):
                    if cond is not None:
                        scores = jnp.where(cond, scores, LOW)
                s_ref[r * nt + t] = scores
                highest = jnp.maximum(highest, jnp.max(scores, axis=0, keepdims=True))
        return highest

    def forward(h, highest):
        grads = qg[h, 1]
        total = jnp.zeros((1, tokens), jnp.float32)
        mixed = jnp.zeros((DH, tokens), jnp.float32)
        for r in range(nr):
            for t in range(nt):
                weights = jnp.exp2(s_ref[r * nt + t] - highest)
                s_ref[r * nt + t] = weights
                total = total + jnp.sum(weights, axis=0, keepdims=True)
                mixed = mixed + lax.dot_general(
                    win[h, r, t, 1], weights.astype(jnp.bfloat16), (((0,), (0,)), ((), ())), preferred_element_type=jnp.float32
                )
        inverse = 1.0 / total
        attended = jnp.transpose(mixed * inverse).astype(jnp.bfloat16)
        outb[h, 0] = attended
        products = grads.astype(jnp.float32) * attended.astype(jnp.float32)
        row_dot = jnp.sum(jnp.transpose(products), axis=0, keepdims=True)
        return inverse, row_dot

    def backward(h, inverse, row_dot, query_grad, rs):
        queries = qg[h, 0]
        grads = qg[h, 1]
        for r in rs:
            for t in reversed(range(nt)):
                keys, values = win[h, r, t, 0], win[h, r, t, 1]
                probs = s_ref[r * nt + t] * inverse
                value_term = jnp.dot(probs.astype(jnp.bfloat16), grads, preferred_element_type=jnp.float32)
                prob_grad = lax.dot_general(values, grads, (((1,), (1,)), ((), ())), preferred_element_type=jnp.float32)
                score_grad = (probs * (prob_grad - row_dot)).astype(jnp.bfloat16)
                query_grad = query_grad + lax.dot_general(
                    keys, score_grad, (((0,), (0,)), ((), ())), preferred_element_type=jnp.float32
                )
                key_term = jnp.dot(score_grad, queries, preferred_element_type=jnp.float32) * factor
                if r == 0:
                    own[h, t, 0] = key_term
                    own[h, t, 1] = value_term
                else:
                    r1s[h, r - 1, t, 0] = key_term.astype(jnp.bfloat16)
                    r1s[h, r - 1, t, 1] = value_term.astype(jnp.bfloat16)
                    valid = sides[r - 1][1]
                    guarded(both(valid, inner) if t == 2 else valid, lambda r=r, t=t: back_side(h, r - 1, t).start())
        return query_grad

    def send_query_grad(h, query_grad):
        outb[h, 1] = jnp.transpose(query_grad * factor).astype(jnp.bfloat16)
        send_out(h, 0)

    def fold_sides(h):
        for t in reversed(range(nt)):
            for i, (peer, valid, _) in enumerate(sides):

                def fold(i=i, t=t):
                    back_from_side(h, i, t).wait_recv()
                    own[h, t] = own[h, t] + r1r[h, i, t].astype(jnp.float32)

                guarded(both(valid, inner) if t == 2 else valid, fold)
            if t > 0:

                def send(t=t):
                    for a in range(2):
                        r2s[h, t - 1, a] = own[h, t, a].astype(jnp.bfloat16)
                        (back_across if t == 2 else back_pair)(h, a).start()

                guarded(inner if relay or t == 2 else None, send)

    def fold_across(h):
        @pl.when(corner if relay else inner)
        def _():
            for a in range(2):
                back_across(h, a).wait_recv()
                if relay:
                    r2s[h, 0, a] = (own[h, 1, a] + r2r[h, 1, a].astype(jnp.float32)).astype(jnp.bfloat16)
                    back_pair(h, a).start()
                else:
                    own[h, 0, a] = own[h, 0, a] + r2r[h, 1, a].astype(jnp.float32)

    def fold_pair(h, send=send_out):
        for a in range(2):
            back_pair(h, a).wait_recv()
            outb[h, a + 2] = (own[h, 0, a] + r2r[h, 0, a].astype(jnp.float32)).astype(jnp.bfloat16)
        send(h, 1)
        for a in range(4):
            out_ref[a, :, columns(z, h)] = outb[h, a, part(z), :]

    def later(h, fn):
        pl.when(h < heads)(lambda: fn(h))

    def earlier(h, fn):
        pl.when(h >= 0)(lambda: fn(h))

    spread_own(0)
    if heads > 2:
        send_kv(2)
    if heads > 1:
        spread_own(1)
        send_qg(1)
    spread_pair(0)
    spread_across(0)

    @pl.loop(0, heads)
    def _(h):
        highest = score(h)
        later(h + 3, send_kv)
        later(h + 1, spread_pair)
        inverse, row_dot = forward(h, highest)
        earlier(h - 2, fold_pair)
        later(h + 2, spread_own)
        later(h + 2, send_qg)
        query_grad = backward(h, inverse, row_dot, jnp.zeros((DH, tokens), jnp.float32), range(nr - 1, 0, -1))
        earlier(h - 1, fold_across)
        query_grad = backward(h, inverse, row_dot, query_grad, (0,))
        send_query_grad(h, query_grad)
        fold_sides(h)
        later(h + 1, spread_across)

    final = range(max(0, heads - 2), heads)
    if heads > 1:
        fold_pair(heads - 2, send_ahead)
    fold_across(heads - 1)
    fold_pair(heads - 1, send_ahead)
    for h in final:
        send_rest(h, 1)

    @pl.loop(0, heads)
    def _(h):
        for p in range(2):
            for d in hops:
                in_copy(h, p, d).wait_send()
                out_copy(h, p, d).wait_recv()
                out_copy(h, p, d).wait_send()
        for a in range(2):
            pair_copy(h, a).wait_send()
            back_pair(h, a).wait_send()
            pl.when(corner if relay else inner)(lambda a=a: across_copy(h, a).wait_send())
            pl.when(inner)(lambda a=a: back_across(h, a).wait_send())
        for i, (peer, valid, _) in enumerate(sides):
            for t in range(nt):

                def drain(i=i, t=t):
                    side_copy(h, i, t).wait_send()
                    back_side(h, i, t).wait_send()

                guarded(both(valid, inner) if t == 2 else valid, drain)


def store(held, *refs):
    sems = refs[4]
    copies = [pltpu.make_async_copy(held.at[i], refs[i], sems.at[i]) for i in range(4)]
    for copy in copies:
        copy.start()
    for copy in copies:
        copy.wait()


def body(queries, keys, values, out_grad):
    sizes = tuple(lax.axis_size(axis) for axis in ("ta", "ha", "head"))
    size_t, size_h, size_z = sizes
    assert size_t % 2 == 0 and size_z & (size_z - 1) == 0
    shape = queries.shape
    rows = shape[0] * shape[1] * shape[2]
    width = shape[3]
    heads = width // DH // size_z
    tokens = rows * size_z
    nt, nr = 3, min(3, size_h)
    bf16 = jnp.bfloat16
    dma = pltpu.SemaphoreType.DMA
    mr = max(1, nr - 1)
    flat = [x.reshape(rows, width) for x in (queries, keys, values, out_grad)]
    held = pl.pallas_call(
        functools.partial(kernel, sizes, rows, heads),
        out_shape=pltpu.VMEM((4, rows, width), bf16),
        in_specs=[pl.BlockSpec(memory_space=pl.ANY)] * 4,
        out_specs=pl.BlockSpec(memory_space=pltpu.VMEM),
        scratch_shapes=[
            pltpu.VMEM((heads, 2, tokens, DH), bf16),
            pltpu.VMEM((heads, nr, nt, 2, tokens, DH), bf16),
            pltpu.VMEM((heads, 2, size_z - 1, 2, rows, DH), bf16),
            pltpu.VMEM((nr * nt, tokens, tokens), jnp.float32),
            pltpu.VMEM((heads, 4, tokens, DH), bf16),
            pltpu.VMEM((heads, nt, 2, tokens, DH), jnp.float32),
            pltpu.VMEM((heads, mr, nt, 2, tokens, DH), bf16),
            pltpu.VMEM((heads, mr, nt, 2, tokens, DH), bf16),
            pltpu.VMEM((heads, 2, 2, tokens, DH), bf16),
            pltpu.VMEM((heads, 2, 2, tokens, DH), bf16),
            dma((heads, 2, size_z)),
            dma((heads, 2, size_z)),
            dma((heads, 2)),
            dma((heads, 2)),
            dma((heads, 2)),
            dma((heads, 2)),
            dma((heads, mr, nt)),
            dma((heads, mr, nt)),
            dma((heads, mr, nt)),
            dma((heads, mr, nt)),
            dma((heads, 2)),
            dma((heads, 2)),
            dma((heads, 2)),
            dma((heads, 2)),
            dma((heads, 2, size_z)),
            dma((heads, 2, size_z)),
            dma((heads, 4)),
            dma((heads, 4, size_z)),
        ],
        compiler_params=pltpu.CompilerParams(collective_id=0, has_side_effects=True, vmem_limit_bytes=56 * 1024 * 1024),
        name="tile_attention",
    )(*flat)
    outs = pl.pallas_call(
        store,
        out_shape=[jax.ShapeDtypeStruct((rows, width), bf16)] * 4,
        in_specs=[pl.BlockSpec(memory_space=pl.ANY)],
        out_specs=[pl.BlockSpec(memory_space=pl.ANY)] * 4,
        scratch_shapes=[dma((4,))],
        name="store",
    )(pltpu.with_memory_space_constraint(held, pltpu.VMEM))
    return tuple(x.reshape(shape) for x in outs)


def solution(mesh):
    spec = P("ta", ("ha", "head"), None, None)
    return jax.shard_map(body, mesh=mesh, in_specs=(spec,) * 4, out_specs=(spec,) * 4, check_vma=False)
```

```python
import functools
import math

import jax
import jax.numpy as jnp
from jax import lax
from jax.experimental import pallas as pl
from jax.experimental.pallas import tpu as pltpu
from jax.sharding import PartitionSpec as P

DH = 128
LOW = -1e30
MESH = pl.DeviceIdType.MESH


def sides_of(axis, size):
    me = lax.axis_index(axis)
    if size == 1:
        return []
    if size == 2:
        return [(1 - me, None, 1)]
    return [(me - 1, me > 0, 2), (me + 1, me < size - 1, 1)]


def guarded(valid, fn):
    if valid is None:
        fn()
    else:
        pl.when(valid)(fn)


def flip(index, bits):
    step = 1
    while step <= bits:
        if bits // step % 2:
            index = index + step - 2 * step * (lax.rem(lax.div(index, step), 2))
        step *= 2
    return index


def differ(one, other, size):
    bits, step = 0, 1
    while step < size:
        bits = bits + step * lax.rem(lax.div(one, step) + lax.div(other, step), 2)
        step *= 2
    return bits


def kernel(
    sizes,
    rows,
    heads,
    q_ref,
    k_ref,
    v_ref,
    g_ref,
    out_ref,
    qg,
    win,
    stage,
    s_ref,
    outb,
    own,
    r1s,
    r1r,
    r2s,
    r2r,
    in_s,
    in_r,
    px_s,
    px_r,
    py_s,
    py_r,
    hc_s,
    hc_r,
    bc_s,
    bc_r,
    bx_s,
    bx_r,
    by_s,
    by_r,
    ou_s,
    ou_r,
    lo_s,
    st_s,
):
    size_t, size_h, size_z = sizes
    tokens = rows * size_z
    z = lax.axis_index("head")
    ta = lax.axis_index("ta")
    corner = (ta == 0) | (ta == size_t - 1)
    inner = jnp.logical_not(corner)
    pair = flip(ta, 1)
    relay = size_t == 4
    across = flip(ta, 2) if relay else ta - 1 + 2 * lax.rem(ta, 2)
    sides = sides_of("ha", size_h)
    nt, nr = 3, 1 + len(sides)
    factor = 1.0 / math.sqrt(DH)
    scale = factor * math.log2(math.e)
    hops = list(range(size_z - 1, 0, -1))

    barrier = pltpu.get_barrier_semaphore()
    expected = size_z
    for d in hops:
        pl.semaphore_signal(barrier, inc=1, device_id={"head": flip(z, d)}, device_id_type=MESH)
    pl.semaphore_signal(barrier, inc=1, device_id={"ta": pair}, device_id_type=MESH)
    for axis, peer, valid in [("ta", across, None if relay else inner)] + [("ha", peer, valid) for peer, valid, _ in sides]:

        def greet(axis=axis, peer=peer):
            pl.semaphore_signal(barrier, inc=1, device_id={axis: peer}, device_id_type=MESH)

        guarded(valid, greet)
        expected = expected + (1 if valid is None else jnp.where(valid, 1, 0))
    def columns(group, h):
        return pl.ds(pl.multiple_of((group * heads + h) * DH, DH), DH)

    def part(group):
        return pl.ds(pl.multiple_of(group * rows, rows), rows)

    ins = (k_ref, v_ref, q_ref, g_ref)

    def remote(src, dst, send, recv, device):
        return pltpu.make_async_remote_copy(
            src_ref=src, dst_ref=dst, send_sem=send, recv_sem=recv, device_id=device, device_id_type=MESH
        )

    def landing(h, p):
        return win.at[h, 0, 0, :, part(z), :] if p == 0 else qg.at[h, :, part(z), :]

    def stage_copy(h, a, d):
        return pltpu.make_async_copy(ins[a].at[:, columns(flip(z, d), h)], stage.at[h, a // 2, d - 1, a % 2], st_s.at[h, a, d])

    def local_copy(h, a):
        return pltpu.make_async_copy(ins[a].at[:, columns(z, h)], landing(h, a // 2).at[a % 2], lo_s.at[h, a])

    def in_copy(h, p, d):
        return remote(stage.at[h, p, d - 1], landing(h, p), in_s.at[h, p, d], in_r.at[h, p, d], {"head": flip(z, d)})

    def out_copy(h, p, d, peer=None):
        peer = flip(z, d) if peer is None else peer
        return remote(
            outb.at[h, pl.ds(2 * p, 2), part(peer), :],
            out_ref.at[pl.ds(2 * p, 2), :, columns(z, h)],
            ou_s.at[h, p, d],
            ou_r.at[h, p, d],
            {"head": peer},
        )

    def pair_copy(h, a):
        return remote(win.at[h, 0, 0, a], win.at[h, 0, 1, a], px_s.at[h, a], px_r.at[h, a], {"ta": pair})

    def across_copy(h, a):
        return remote(win.at[h, 0, 1 if relay else 0, a], win.at[h, 0, 2, a], py_s.at[h, a], py_r.at[h, a], {"ta": across})

    def side_copy(h, i, t):
        peer, _, there = sides[i]
        return remote(win.at[h, 0, t], win.at[h, there, t], hc_s.at[h, i, t], hc_r.at[h, there - 1, t], {"ha": peer})

    def back_side(h, i, t):
        peer, _, there = sides[i]
        return remote(r1s.at[h, i, t], r1r.at[h, there - 1, t], bc_s.at[h, i, t], bc_r.at[h, there - 1, t], {"ha": peer})

    def back_pair(h, a):
        return remote(r2s.at[h, 0, a], r2r.at[h, 0, a], bx_s.at[h, a], bx_r.at[h, a], {"ta": pair})

    def back_across(h, a):
        return remote(r2s.at[h, 1, a], r2r.at[h, 1, a], by_s.at[h, a], by_r.at[h, a], {"ta": across})

    def from_side(h, i, t):
        peer = sides[i][0]
        return remote(win.at[h, i + 1, t], win.at[h, i + 1, t], hc_r.at[h, i, t], hc_r.at[h, i, t], {"ha": peer})

    def back_from_side(h, i, t):
        peer = sides[i][0]
        return remote(r1r.at[h, i, t], r1r.at[h, i, t], bc_r.at[h, i, t], bc_r.at[h, i, t], {"ha": peer})

    def both(valid, other):
        return other if valid is None else valid & other

    def send_in(h, p):
        for d in hops:
            for a in (2 * p, 2 * p + 1):
                stage_copy(h, a, d).wait()
            in_copy(h, p, d).start()

    def send_kv(h):
        send_in(h, 0)

    def send_qg(h):
        send_in(h, 1)

    def send_step(h, p, i):
        peer = jnp.where(z == 0, size_z - 1 - i, jnp.where(i >= z, i + 1, i))
        out_copy(h, p, differ(z, peer, size_z), peer).start()

    def send_out(h, p):
        for i in range(size_z - 1):
            send_step(h, p, i)

    def send_ahead(h, p):
        send_step(h, p, 0)

        @pl.when(z == 0)
        def _():
            for i in range(1, size_z - 1):
                send_step(h, p, i)

    def send_rest(h, p):
        @pl.when(z != 0)
        def _():
            for i in range(1, size_z - 1):
                send_step(h, p, i)

    def fetch(h, p):
        for a in (2 * p, 2 * p + 1):
            for d in hops:
                stage_copy(h, a, d).start()
        for a in (2 * p, 2 * p + 1):
            local_copy(h, a).start()

    fetch(0, 0)
    pl.semaphore_wait(barrier, expected)
    send_kv(0)
    if heads > 1:
        fetch(1, 0)
    fetch(0, 1)
    if heads > 1:
        send_kv(1)
    send_qg(0)
    for h in range(2, heads):
        fetch(h, 0)
    for h in range(1, heads):
        fetch(h, 1)

    @pl.when(corner)
    def _():
        @pl.loop(0, heads)
        def _(h):
            for r in range(nr):
                win[h, r, 2] = jnp.zeros((2, tokens, DH), win.dtype)

    for i, (peer, valid, _) in enumerate(sides):
        if valid is not None:

            @pl.when(jnp.logical_not(valid))
            def _(i=i):
                @pl.loop(0, heads)
                def _(h):
                    win[h, i + 1] = jnp.zeros((nt, 2, tokens, DH), win.dtype)


    def to_sides(h, t, cond=None):
        for i, (peer, valid, _) in enumerate(sides):
            go = valid if cond is None else both(valid, cond)
            guarded(go, lambda i=i: side_copy(h, i, t).start())

    def spread_own(h):
        for d in hops:
            in_copy(h, 0, d).wait_recv()
        for a in range(2):
            local_copy(h, a).wait()
            pair_copy(h, a).start()
            if not relay:
                pl.when(inner)(lambda a=a: across_copy(h, a).start())
        to_sides(h, 0)

    def spread_pair(h):
        for a in range(2):
            pair_copy(h, a).wait_recv()
            if relay:
                pl.when(corner)(lambda a=a: across_copy(h, a).start())
        to_sides(h, 1)

    def spread_across(h):
        @pl.when(inner)
        def _():
            for a in range(2):
                across_copy(h, a).wait_recv()
            to_sides(h, 2)

    def score(h):
        for d in hops:
            in_copy(h, 1, d).wait_recv()
        for a in range(2, 4):
            local_copy(h, a).wait()
        queries = qg[h, 0]
        highest = jnp.full((1, tokens), LOW, jnp.float32)
        for r in range(nr):
            for t in range(nt):
                if r > 0:
                    valid = sides[r - 1][1]
                    guarded(both(valid, inner) if t == 2 else valid, lambda r=r, t=t: from_side(h, r - 1, t).wait_recv())
                scores = lax.dot_general(win[h, r, t, 0], queries, (((1,), (1,)), ((), ())), preferred_element_type=jnp.float32) * scale
                for cond in ([inner] if t == 2 else []) + ([sides[r - 1][1]] if r > 0 else []):
                    if cond is not None:
                        scores = jnp.where(cond, scores, LOW)
                s_ref[r * nt + t] = scores
                highest = jnp.maximum(highest, jnp.max(scores, axis=0, keepdims=True))
        return highest

    def forward(h, highest):
        grads = qg[h, 1]
        total = jnp.zeros((1, tokens), jnp.float32)
        mixed = jnp.zeros((DH, tokens), jnp.float32)
        for r in range(nr):
            for t in range(nt):
                weights = jnp.exp2(s_ref[r * nt + t] - highest)
                s_ref[r * nt + t] = weights
                total = total + jnp.sum(weights, axis=0, keepdims=True)
                mixed = mixed + lax.dot_general(
                    win[h, r, t, 1], weights.astype(jnp.bfloat16), (((0,), (0,)), ((), ())), preferred_element_type=jnp.float32
                )
        inverse = 1.0 / total
        attended = jnp.transpose(mixed * inverse).astype(jnp.bfloat16)
        outb[h, 0] = attended
        products = grads.astype(jnp.float32) * attended.astype(jnp.float32)
        row_dot = jnp.sum(jnp.transpose(products), axis=0, keepdims=True)
        return inverse, row_dot

    def backward(h, inverse, row_dot, query_grad, rs):
        queries = qg[h, 0]
        grads = qg[h, 1]
        for r in rs:
            for t in reversed(range(nt)):
                keys, values = win[h, r, t, 0], win[h, r, t, 1]
                probs = s_ref[r * nt + t] * inverse
                value_term = jnp.dot(probs.astype(jnp.bfloat16), grads, preferred_element_type=jnp.float32)
                prob_grad = lax.dot_general(values, grads, (((1,), (1,)), ((), ())), preferred_element_type=jnp.float32)
                score_grad = (probs * (prob_grad - row_dot)).astype(jnp.bfloat16)
                query_grad = query_grad + lax.dot_general(
                    keys, score_grad, (((0,), (0,)), ((), ())), preferred_element_type=jnp.float32
                )
                key_term = jnp.dot(score_grad, queries, preferred_element_type=jnp.float32) * factor
                if r == 0:
                    own[h, t, 0] = key_term
                    own[h, t, 1] = value_term
                else:
                    r1s[h, r - 1, t, 0] = key_term.astype(jnp.bfloat16)
                    r1s[h, r - 1, t, 1] = value_term.astype(jnp.bfloat16)
                    valid = sides[r - 1][1]
                    guarded(both(valid, inner) if t == 2 else valid, lambda r=r, t=t: back_side(h, r - 1, t).start())
        return query_grad

    def send_query_grad(h, query_grad):
        outb[h, 1] = jnp.transpose(query_grad * factor).astype(jnp.bfloat16)
        keep = corner & (h == heads - 1)
        pl.when(keep)(lambda: send_ahead(h, 0))
        pl.when(jnp.logical_not(keep))(lambda: send_out(h, 0))

    def fold_sides(h):
        for t in reversed(range(nt)):
            for i, (peer, valid, _) in enumerate(sides):

                def fold(i=i, t=t):
                    back_from_side(h, i, t).wait_recv()
                    own[h, t] = own[h, t] + r1r[h, i, t].astype(jnp.float32)

                guarded(both(valid, inner) if t == 2 else valid, fold)
            if t > 0:

                def send(t=t):
                    for a in range(2):
                        r2s[h, t - 1, a] = own[h, t, a].astype(jnp.bfloat16)
                        (back_across if t == 2 else back_pair)(h, a).start()

                guarded(inner if relay or t == 2 else None, send)

    def fold_across(h):
        @pl.when(corner if relay else inner)
        def _():
            for a in range(2):
                back_across(h, a).wait_recv()
                if relay:
                    r2s[h, 0, a] = (own[h, 1, a] + r2r[h, 1, a].astype(jnp.float32)).astype(jnp.bfloat16)
                    back_pair(h, a).start()
                else:
                    own[h, 0, a] = own[h, 0, a] + r2r[h, 1, a].astype(jnp.float32)

    def fold_pair(h, send=send_out):
        for a in range(2):
            back_pair(h, a).wait_recv()
            outb[h, a + 2] = (own[h, 0, a] + r2r[h, 0, a].astype(jnp.float32)).astype(jnp.bfloat16)
        send(h, 1)
        for a in range(4):
            out_ref[a, :, columns(z, h)] = outb[h, a, part(z), :]

    def later(h, fn):
        pl.when(h < heads)(lambda: fn(h))

    def earlier(h, fn):
        pl.when(h >= 0)(lambda: fn(h))

    spread_own(0)
    if heads > 2:
        send_kv(2)
    if heads > 1:
        spread_own(1)
        send_qg(1)
    spread_pair(0)
    spread_across(0)

    @pl.loop(0, heads)
    def _(h):
        highest = score(h)
        later(h + 3, send_kv)
        later(h + 1, spread_pair)
        inverse, row_dot = forward(h, highest)
        earlier(h - 2, fold_pair)
        later(h + 2, spread_own)
        later(h + 2, send_qg)
        query_grad = backward(h, inverse, row_dot, jnp.zeros((DH, tokens), jnp.float32), range(nr - 1, 0, -1))
        earlier(h - 1, fold_across)
        query_grad = backward(h, inverse, row_dot, query_grad, (0,))
        send_query_grad(h, query_grad)
        fold_sides(h)
        later(h + 1, spread_across)

    final = range(max(0, heads - 2), heads)
    if heads > 1:
        fold_pair(heads - 2, send_ahead)
    fold_across(heads - 1)
    fold_pair(heads - 1, send_ahead)
    pl.when(corner)(lambda: send_rest(heads - 1, 0))
    for h in final:
        send_rest(h, 1)

    @pl.loop(0, heads)
    def _(h):
        for p in range(2):
            for d in hops:
                in_copy(h, p, d).wait_send()
                out_copy(h, p, d).wait_recv()
                out_copy(h, p, d).wait_send()
        for a in range(2):
            pair_copy(h, a).wait_send()
            back_pair(h, a).wait_send()
            pl.when(corner if relay else inner)(lambda a=a: across_copy(h, a).wait_send())
            pl.when(inner)(lambda a=a: back_across(h, a).wait_send())
        for i, (peer, valid, _) in enumerate(sides):
            for t in range(nt):

                def drain(i=i, t=t):
                    side_copy(h, i, t).wait_send()
                    back_side(h, i, t).wait_send()

                guarded(both(valid, inner) if t == 2 else valid, drain)


def store(held, *refs):
    sems = refs[4]
    copies = [pltpu.make_async_copy(held.at[i], refs[i], sems.at[i]) for i in range(4)]
    for copy in copies:
        copy.start()
    for copy in copies:
        copy.wait()


def body(queries, keys, values, out_grad):
    sizes = tuple(lax.axis_size(axis) for axis in ("ta", "ha", "head"))
    size_t, size_h, size_z = sizes
    assert size_t % 2 == 0 and size_z & (size_z - 1) == 0
    shape = queries.shape
    rows = shape[0] * shape[1] * shape[2]
    width = shape[3]
    heads = width // DH // size_z
    tokens = rows * size_z
    nt, nr = 3, min(3, size_h)
    bf16 = jnp.bfloat16
    dma = pltpu.SemaphoreType.DMA
    mr = max(1, nr - 1)
    flat = [x.reshape(rows, width) for x in (queries, keys, values, out_grad)]
    held = pl.pallas_call(
        functools.partial(kernel, sizes, rows, heads),
        out_shape=pltpu.VMEM((4, rows, width), bf16),
        in_specs=[pl.BlockSpec(memory_space=pl.ANY)] * 4,
        out_specs=pl.BlockSpec(memory_space=pltpu.VMEM),
        scratch_shapes=[
            pltpu.VMEM((heads, 2, tokens, DH), bf16),
            pltpu.VMEM((heads, nr, nt, 2, tokens, DH), bf16),
            pltpu.VMEM((heads, 2, size_z - 1, 2, rows, DH), bf16),
            pltpu.VMEM((nr * nt, tokens, tokens), jnp.float32),
            pltpu.VMEM((heads, 4, tokens, DH), bf16),
            pltpu.VMEM((heads, nt, 2, tokens, DH), jnp.float32),
            pltpu.VMEM((heads, mr, nt, 2, tokens, DH), bf16),
            pltpu.VMEM((heads, mr, nt, 2, tokens, DH), bf16),
            pltpu.VMEM((heads, 2, 2, tokens, DH), bf16),
            pltpu.VMEM((heads, 2, 2, tokens, DH), bf16),
            dma((heads, 2, size_z)),
            dma((heads, 2, size_z)),
            dma((heads, 2)),
            dma((heads, 2)),
            dma((heads, 2)),
            dma((heads, 2)),
            dma((heads, mr, nt)),
            dma((heads, mr, nt)),
            dma((heads, mr, nt)),
            dma((heads, mr, nt)),
            dma((heads, 2)),
            dma((heads, 2)),
            dma((heads, 2)),
            dma((heads, 2)),
            dma((heads, 2, size_z)),
            dma((heads, 2, size_z)),
            dma((heads, 4)),
            dma((heads, 4, size_z)),
        ],
        compiler_params=pltpu.CompilerParams(collective_id=0, has_side_effects=True, vmem_limit_bytes=56 * 1024 * 1024),
        name="tile_attention",
    )(*flat)
    outs = pl.pallas_call(
        store,
        out_shape=[jax.ShapeDtypeStruct((rows, width), bf16)] * 4,
        in_specs=[pl.BlockSpec(memory_space=pl.ANY)],
        out_specs=[pl.BlockSpec(memory_space=pl.ANY)] * 4,
        scratch_shapes=[dma((4,))],
        name="store",
    )(pltpu.with_memory_space_constraint(held, pltpu.VMEM))
    return tuple(x.reshape(shape) for x in outs)


def solution(mesh):
    spec = P("ta", ("ha", "head"), None, None)
    return jax.shard_map(body, mesh=mesh, in_specs=(spec,) * 4, out_specs=(spec,) * 4, check_vma=False)
```

```python
import functools
import math

import jax
import jax.numpy as jnp
from jax import lax
from jax.experimental import pallas as pl
from jax.experimental.pallas import tpu as pltpu
from jax.sharding import PartitionSpec as P

DH = 128
LOW = -1e30
MESH = pl.DeviceIdType.MESH


def sides_of(axis, size):
    me = lax.axis_index(axis)
    if size == 1:
        return []
    if size == 2:
        return [(1 - me, None, 1)]
    return [(me - 1, me > 0, 2), (me + 1, me < size - 1, 1)]


def guarded(valid, fn):
    if valid is None:
        fn()
    else:
        pl.when(valid)(fn)


def flip(index, bits):
    step = 1
    while step <= bits:
        if bits // step % 2:
            index = index + step - 2 * step * (lax.rem(lax.div(index, step), 2))
        step *= 2
    return index


def differ(one, other, size):
    bits, step = 0, 1
    while step < size:
        bits = bits + step * lax.rem(lax.div(one, step) + lax.div(other, step), 2)
        step *= 2
    return bits


def kernel(
    sizes,
    rows,
    heads,
    q_ref,
    k_ref,
    v_ref,
    g_ref,
    out_ref,
    qg,
    win,
    stage,
    s_ref,
    outb,
    own,
    r1s,
    r1r,
    r2s,
    r2r,
    in_s,
    in_r,
    px_s,
    px_r,
    py_s,
    py_r,
    hc_s,
    hc_r,
    bc_s,
    bc_r,
    bx_s,
    bx_r,
    by_s,
    by_r,
    ou_s,
    ou_r,
    lo_s,
    st_s,
):
    size_t, size_h, size_z = sizes
    tokens = rows * size_z
    z = lax.axis_index("head")
    ta = lax.axis_index("ta")
    corner = (ta == 0) | (ta == size_t - 1)
    inner = jnp.logical_not(corner)
    pair = flip(ta, 1)
    relay = size_t == 4
    across = flip(ta, 2) if relay else ta - 1 + 2 * lax.rem(ta, 2)
    sides = sides_of("ha", size_h)
    nt, nr = 3, 1 + len(sides)
    factor = 1.0 / math.sqrt(DH)
    scale = factor * math.log2(math.e)
    hops = list(range(size_z - 1, 0, -1))

    barrier = pltpu.get_barrier_semaphore()
    expected = size_z
    for d in hops:
        pl.semaphore_signal(barrier, inc=1, device_id={"head": flip(z, d)}, device_id_type=MESH)
    pl.semaphore_signal(barrier, inc=1, device_id={"ta": pair}, device_id_type=MESH)
    for axis, peer, valid in [("ta", across, None if relay else inner)] + [("ha", peer, valid) for peer, valid, _ in sides]:

        def greet(axis=axis, peer=peer):
            pl.semaphore_signal(barrier, inc=1, device_id={axis: peer}, device_id_type=MESH)

        guarded(valid, greet)
        expected = expected + (1 if valid is None else jnp.where(valid, 1, 0))
    def columns(group, h):
        return pl.ds(pl.multiple_of((group * heads + h) * DH, DH), DH)

    def part(group):
        return pl.ds(pl.multiple_of(group * rows, rows), rows)

    ins = (k_ref, v_ref, q_ref, g_ref)

    def remote(src, dst, send, recv, device):
        return pltpu.make_async_remote_copy(
            src_ref=src, dst_ref=dst, send_sem=send, recv_sem=recv, device_id=device, device_id_type=MESH
        )

    def landing(h, p):
        return win.at[h, 0, 0, :, part(z), :] if p == 0 else qg.at[h, :, part(z), :]

    def stage_copy(h, a, d):
        return pltpu.make_async_copy(ins[a].at[:, columns(flip(z, d), h)], stage.at[h, a // 2, d - 1, a % 2], st_s.at[h, a, d])

    def local_copy(h, a):
        return pltpu.make_async_copy(ins[a].at[:, columns(z, h)], landing(h, a // 2).at[a % 2], lo_s.at[h, a])

    def in_copy(h, p, d):
        return remote(stage.at[h, p, d - 1], landing(h, p), in_s.at[h, p, d], in_r.at[h, p, d], {"head": flip(z, d)})

    def out_copy(h, p, d, peer=None):
        peer = flip(z, d) if peer is None else peer
        return remote(
            outb.at[h, pl.ds(2 * p, 2), part(peer), :],
            out_ref.at[pl.ds(2 * p, 2), :, columns(z, h)],
            ou_s.at[h, p, d],
            ou_r.at[h, p, d],
            {"head": peer},
        )

    def pair_copy(h, a):
        return remote(win.at[h, 0, 0, a], win.at[h, 0, 1, a], px_s.at[h, a], px_r.at[h, a], {"ta": pair})

    def across_copy(h, a):
        return remote(win.at[h, 0, 1 if relay else 0, a], win.at[h, 0, 2, a], py_s.at[h, a], py_r.at[h, a], {"ta": across})

    def side_copy(h, i, t):
        peer, _, there = sides[i]
        return remote(win.at[h, 0, t], win.at[h, there, t], hc_s.at[h, i, t], hc_r.at[h, there - 1, t], {"ha": peer})

    def back_side(h, i, t):
        peer, _, there = sides[i]
        return remote(r1s.at[h, i, t], r1r.at[h, there - 1, t], bc_s.at[h, i, t], bc_r.at[h, there - 1, t], {"ha": peer})

    def back_pair(h, a):
        return remote(r2s.at[h, 0, a], r2r.at[h, 0, a], bx_s.at[h, a], bx_r.at[h, a], {"ta": pair})

    def back_across(h, a):
        return remote(r2s.at[h, 1, a], r2r.at[h, 1, a], by_s.at[h, a], by_r.at[h, a], {"ta": across})

    def from_side(h, i, t):
        peer = sides[i][0]
        return remote(win.at[h, i + 1, t], win.at[h, i + 1, t], hc_r.at[h, i, t], hc_r.at[h, i, t], {"ha": peer})

    def back_from_side(h, i, t):
        peer = sides[i][0]
        return remote(r1r.at[h, i, t], r1r.at[h, i, t], bc_r.at[h, i, t], bc_r.at[h, i, t], {"ha": peer})

    def both(valid, other):
        return other if valid is None else valid & other

    def send_in(h, p):
        for d in hops:
            for a in (2 * p, 2 * p + 1):
                stage_copy(h, a, d).wait()
            in_copy(h, p, d).start()

    def send_kv(h):
        send_in(h, 0)

    def send_qg(h):
        send_in(h, 1)

    def send_step(h, p, i):
        peer = jnp.where(z == 0, size_z - 1 - i, jnp.where(i >= z, i + 1, i))
        out_copy(h, p, differ(z, peer, size_z), peer).start()

    def send_out(h, p):
        for i in range(size_z - 1):
            send_step(h, p, i)

    def send_ahead(h, p):
        send_step(h, p, 0)

        @pl.when(z == 0)
        def _():
            for i in range(1, size_z - 1):
                send_step(h, p, i)

    def send_rest(h, p):
        @pl.when(z != 0)
        def _():
            for i in range(1, size_z - 1):
                send_step(h, p, i)

    def fetch(h, p):
        for a in (2 * p, 2 * p + 1):
            for d in hops:
                stage_copy(h, a, d).start()
        for a in (2 * p, 2 * p + 1):
            local_copy(h, a).start()

    fetch(0, 0)
    pl.semaphore_wait(barrier, expected)
    send_kv(0)
    if heads > 1:
        fetch(1, 0)
    fetch(0, 1)
    if heads > 1:
        send_kv(1)
    send_qg(0)
    for h in range(2, heads):
        fetch(h, 0)
    for h in range(1, heads):
        fetch(h, 1)

    @pl.when(corner)
    def _():
        @pl.loop(0, heads)
        def _(h):
            for r in range(nr):
                win[h, r, 2] = jnp.zeros((2, tokens, DH), win.dtype)

    for i, (peer, valid, _) in enumerate(sides):
        if valid is not None:

            @pl.when(jnp.logical_not(valid))
            def _(i=i):
                @pl.loop(0, heads)
                def _(h):
                    win[h, i + 1] = jnp.zeros((nt, 2, tokens, DH), win.dtype)


    def to_sides(h, t, cond=None):
        for i, (peer, valid, _) in enumerate(sides):
            go = valid if cond is None else both(valid, cond)
            guarded(go, lambda i=i: side_copy(h, i, t).start())

    def spread_own(h):
        for d in hops:
            in_copy(h, 0, d).wait_recv()
        for a in range(2):
            local_copy(h, a).wait()
            pair_copy(h, a).start()
            if not relay:
                pl.when(inner)(lambda a=a: across_copy(h, a).start())
        to_sides(h, 0)

    def spread_pair(h):
        for a in range(2):
            pair_copy(h, a).wait_recv()
            if relay:
                pl.when(corner)(lambda a=a: across_copy(h, a).start())
        to_sides(h, 1)

    def spread_across(h):
        @pl.when(inner)
        def _():
            for a in range(2):
                across_copy(h, a).wait_recv()
            to_sides(h, 2)

    def score(h):
        for d in hops:
            in_copy(h, 1, d).wait_recv()
        for a in range(2, 4):
            local_copy(h, a).wait()
        queries = qg[h, 0]
        highest = jnp.full((1, tokens), LOW, jnp.float32)
        for r in range(nr):
            for t in range(nt):
                if r > 0:
                    valid = sides[r - 1][1]
                    guarded(both(valid, inner) if t == 2 else valid, lambda r=r, t=t: from_side(h, r - 1, t).wait_recv())
                scores = lax.dot_general(win[h, r, t, 0], queries, (((1,), (1,)), ((), ())), preferred_element_type=jnp.float32) * scale
                for cond in ([inner] if t == 2 else []) + ([sides[r - 1][1]] if r > 0 else []):
                    if cond is not None:
                        scores = jnp.where(cond, scores, LOW)
                s_ref[r * nt + t] = scores
                highest = jnp.maximum(highest, jnp.max(scores, axis=0, keepdims=True))
        return highest

    def forward(h, highest):
        grads = qg[h, 1]
        total = jnp.zeros((1, tokens), jnp.float32)
        mixed = jnp.zeros((DH, tokens), jnp.float32)
        for r in range(nr):
            for t in range(nt):
                weights = jnp.exp2(s_ref[r * nt + t] - highest)
                s_ref[r * nt + t] = weights
                total = total + jnp.sum(weights, axis=0, keepdims=True)
                mixed = mixed + lax.dot_general(
                    win[h, r, t, 1], weights.astype(jnp.bfloat16), (((0,), (0,)), ((), ())), preferred_element_type=jnp.float32
                )
        inverse = 1.0 / total
        attended = jnp.transpose(mixed * inverse).astype(jnp.bfloat16)
        outb[h, 0] = attended
        products = grads.astype(jnp.float32) * attended.astype(jnp.float32)
        row_dot = jnp.sum(jnp.transpose(products), axis=0, keepdims=True)
        return inverse, row_dot

    def fold_sides(h, t):
        for i, (peer, valid, _) in enumerate(sides):

            def fold(i=i, t=t):
                back_from_side(h, i, t).wait_recv()
                own[h, t] = own[h, t] + r1r[h, i, t].astype(jnp.float32)

            guarded(both(valid, inner) if t == 2 else valid, fold)
        if t > 0:

            def send(t=t):
                for a in range(2):
                    r2s[h, t - 1, a] = own[h, t, a].astype(jnp.bfloat16)
                    (back_across if t == 2 else back_pair)(h, a).start()

            guarded(inner if relay or t == 2 else None, send)

    def backward(h, inverse, row_dot, query_grad, rs):
        queries = qg[h, 0]
        grads = qg[h, 1]
        for r in rs:
            for t in reversed(range(nt)):
                keys, values = win[h, r, t, 0], win[h, r, t, 1]
                probs = s_ref[r * nt + t] * inverse
                value_term = jnp.dot(probs.astype(jnp.bfloat16), grads, preferred_element_type=jnp.float32)
                prob_grad = lax.dot_general(values, grads, (((1,), (1,)), ((), ())), preferred_element_type=jnp.float32)
                score_grad = (probs * (prob_grad - row_dot)).astype(jnp.bfloat16)
                query_grad = query_grad + lax.dot_general(
                    keys, score_grad, (((0,), (0,)), ((), ())), preferred_element_type=jnp.float32
                )
                key_term = jnp.dot(score_grad, queries, preferred_element_type=jnp.float32) * factor
                if r == 0:
                    own[h, t, 0] = key_term
                    own[h, t, 1] = value_term
                    fold_sides(h, t)
                else:
                    r1s[h, r - 1, t, 0] = key_term.astype(jnp.bfloat16)
                    r1s[h, r - 1, t, 1] = value_term.astype(jnp.bfloat16)
                    valid = sides[r - 1][1]
                    guarded(both(valid, inner) if t == 2 else valid, lambda r=r, t=t: back_side(h, r - 1, t).start())
        return query_grad

    def send_query_grad(h, query_grad):
        outb[h, 1] = jnp.transpose(query_grad * factor).astype(jnp.bfloat16)
        keep = corner & (h == heads - 1)
        pl.when(keep)(lambda: send_ahead(h, 0))
        pl.when(jnp.logical_not(keep))(lambda: send_out(h, 0))

    def fold_across(h):
        @pl.when(corner if relay else inner)
        def _():
            for a in range(2):
                back_across(h, a).wait_recv()
                if relay:
                    r2s[h, 0, a] = (own[h, 1, a] + r2r[h, 1, a].astype(jnp.float32)).astype(jnp.bfloat16)
                    back_pair(h, a).start()
                else:
                    own[h, 0, a] = own[h, 0, a] + r2r[h, 1, a].astype(jnp.float32)

    def fold_pair(h, send=send_out):
        for a in range(2):
            back_pair(h, a).wait_recv()
            outb[h, a + 2] = (own[h, 0, a] + r2r[h, 0, a].astype(jnp.float32)).astype(jnp.bfloat16)
        send(h, 1)
        for a in range(4):
            out_ref[a, :, columns(z, h)] = outb[h, a, part(z), :]

    def later(h, fn):
        pl.when(h < heads)(lambda: fn(h))

    def earlier(h, fn):
        pl.when(h >= 0)(lambda: fn(h))

    spread_own(0)
    if heads > 2:
        send_kv(2)
    if heads > 1:
        spread_own(1)
        send_qg(1)
    spread_pair(0)
    spread_across(0)

    @pl.loop(0, heads)
    def _(h):
        highest = score(h)
        later(h + 3, send_kv)
        later(h + 1, spread_pair)
        inverse, row_dot = forward(h, highest)
        earlier(h - 2, fold_pair)
        later(h + 2, spread_own)
        later(h + 2, send_qg)
        query_grad = backward(h, inverse, row_dot, jnp.zeros((DH, tokens), jnp.float32), range(nr - 1, 0, -1))
        earlier(h - 1, fold_across)
        query_grad = backward(h, inverse, row_dot, query_grad, (0,))
        send_query_grad(h, query_grad)
        later(h + 1, spread_across)

    final = range(max(0, heads - 2), heads)
    if heads > 1:
        fold_pair(heads - 2, send_ahead)
    fold_across(heads - 1)
    fold_pair(heads - 1, send_ahead)
    pl.when(corner)(lambda: send_rest(heads - 1, 0))
    for h in final:
        send_rest(h, 1)

    @pl.loop(0, heads)
    def _(h):
        for p in range(2):
            for d in hops:
                in_copy(h, p, d).wait_send()
                out_copy(h, p, d).wait_recv()
                out_copy(h, p, d).wait_send()
        for a in range(2):
            pair_copy(h, a).wait_send()
            back_pair(h, a).wait_send()
            pl.when(corner if relay else inner)(lambda a=a: across_copy(h, a).wait_send())
            pl.when(inner)(lambda a=a: back_across(h, a).wait_send())
        for i, (peer, valid, _) in enumerate(sides):
            for t in range(nt):

                def drain(i=i, t=t):
                    side_copy(h, i, t).wait_send()
                    back_side(h, i, t).wait_send()

                guarded(both(valid, inner) if t == 2 else valid, drain)


def store(held, *refs):
    sems = refs[4]
    copies = [pltpu.make_async_copy(held.at[i], refs[i], sems.at[i]) for i in range(4)]
    for copy in copies:
        copy.start()
    for copy in copies:
        copy.wait()


def body(queries, keys, values, out_grad):
    sizes = tuple(lax.axis_size(axis) for axis in ("ta", "ha", "head"))
    size_t, size_h, size_z = sizes
    assert size_t % 2 == 0 and size_z & (size_z - 1) == 0
    shape = queries.shape
    rows = shape[0] * shape[1] * shape[2]
    width = shape[3]
    heads = width // DH // size_z
    tokens = rows * size_z
    nt, nr = 3, min(3, size_h)
    bf16 = jnp.bfloat16
    dma = pltpu.SemaphoreType.DMA
    mr = max(1, nr - 1)
    flat = [x.reshape(rows, width) for x in (queries, keys, values, out_grad)]
    held = pl.pallas_call(
        functools.partial(kernel, sizes, rows, heads),
        out_shape=pltpu.VMEM((4, rows, width), bf16),
        in_specs=[pl.BlockSpec(memory_space=pl.ANY)] * 4,
        out_specs=pl.BlockSpec(memory_space=pltpu.VMEM),
        scratch_shapes=[
            pltpu.VMEM((heads, 2, tokens, DH), bf16),
            pltpu.VMEM((heads, nr, nt, 2, tokens, DH), bf16),
            pltpu.VMEM((heads, 2, size_z - 1, 2, rows, DH), bf16),
            pltpu.VMEM((nr * nt, tokens, tokens), jnp.float32),
            pltpu.VMEM((heads, 4, tokens, DH), bf16),
            pltpu.VMEM((heads, nt, 2, tokens, DH), jnp.float32),
            pltpu.VMEM((heads, mr, nt, 2, tokens, DH), bf16),
            pltpu.VMEM((heads, mr, nt, 2, tokens, DH), bf16),
            pltpu.VMEM((heads, 2, 2, tokens, DH), bf16),
            pltpu.VMEM((heads, 2, 2, tokens, DH), bf16),
            dma((heads, 2, size_z)),
            dma((heads, 2, size_z)),
            dma((heads, 2)),
            dma((heads, 2)),
            dma((heads, 2)),
            dma((heads, 2)),
            dma((heads, mr, nt)),
            dma((heads, mr, nt)),
            dma((heads, mr, nt)),
            dma((heads, mr, nt)),
            dma((heads, 2)),
            dma((heads, 2)),
            dma((heads, 2)),
            dma((heads, 2)),
            dma((heads, 2, size_z)),
            dma((heads, 2, size_z)),
            dma((heads, 4)),
            dma((heads, 4, size_z)),
        ],
        compiler_params=pltpu.CompilerParams(collective_id=0, has_side_effects=True, vmem_limit_bytes=56 * 1024 * 1024),
        name="tile_attention",
    )(*flat)
    outs = pl.pallas_call(
        store,
        out_shape=[jax.ShapeDtypeStruct((rows, width), bf16)] * 4,
        in_specs=[pl.BlockSpec(memory_space=pl.ANY)],
        out_specs=[pl.BlockSpec(memory_space=pl.ANY)] * 4,
        scratch_shapes=[dma((4,))],
        name="store",
    )(pltpu.with_memory_space_constraint(held, pltpu.VMEM))
    return tuple(x.reshape(shape) for x in outs)


def solution(mesh):
    spec = P("ta", ("ha", "head"), None, None)
    return jax.shard_map(body, mesh=mesh, in_specs=(spec,) * 4, out_specs=(spec,) * 4, check_vma=False)
```

```python
import functools
import math

import jax
import jax.numpy as jnp
from jax import lax
from jax.experimental import pallas as pl
from jax.experimental.pallas import tpu as pltpu
from jax.sharding import PartitionSpec as P

DH = 128
LOW = -1e30
MESH = pl.DeviceIdType.MESH


def sides_of(axis, size):
    me = lax.axis_index(axis)
    if size == 1:
        return []
    if size == 2:
        return [(1 - me, None, 1)]
    return [(me - 1, me > 0, 2), (me + 1, me < size - 1, 1)]


def guarded(valid, fn):
    if valid is None:
        fn()
    else:
        pl.when(valid)(fn)


def flip(index, bits):
    step = 1
    while step <= bits:
        if bits // step % 2:
            index = index + step - 2 * step * (lax.rem(lax.div(index, step), 2))
        step *= 2
    return index


def differ(one, other, size):
    bits, step = 0, 1
    while step < size:
        bits = bits + step * lax.rem(lax.div(one, step) + lax.div(other, step), 2)
        step *= 2
    return bits


def kernel(
    sizes,
    rows,
    heads,
    q_ref,
    k_ref,
    v_ref,
    g_ref,
    out_ref,
    qg,
    win,
    stage,
    s_ref,
    outb,
    own,
    r1s,
    r1r,
    r2s,
    r2r,
    in_s,
    in_r,
    px_s,
    px_r,
    py_s,
    py_r,
    hc_s,
    hc_r,
    bc_s,
    bc_r,
    bx_s,
    bx_r,
    by_s,
    by_r,
    ou_s,
    ou_r,
    lo_s,
    st_s,
):
    size_t, size_h, size_z = sizes
    tokens = rows * size_z
    z = lax.axis_index("head")
    ta = lax.axis_index("ta")
    corner = (ta == 0) | (ta == size_t - 1)
    inner = jnp.logical_not(corner)
    pair = flip(ta, 1)
    relay = size_t == 4
    across = flip(ta, 2) if relay else ta - 1 + 2 * lax.rem(ta, 2)
    sides = sides_of("ha", size_h)
    nt, nr = 3, 1 + len(sides)
    factor = 1.0 / math.sqrt(DH)
    scale = factor * math.log2(math.e)
    hops = list(range(size_z - 1, 0, -1))

    barrier = pltpu.get_barrier_semaphore()
    expected = size_z
    for d in hops:
        pl.semaphore_signal(barrier, inc=1, device_id={"head": flip(z, d)}, device_id_type=MESH)
    pl.semaphore_signal(barrier, inc=1, device_id={"ta": pair}, device_id_type=MESH)
    for axis, peer, valid in [("ta", across, None if relay else inner)] + [("ha", peer, valid) for peer, valid, _ in sides]:

        def greet(axis=axis, peer=peer):
            pl.semaphore_signal(barrier, inc=1, device_id={axis: peer}, device_id_type=MESH)

        guarded(valid, greet)
        expected = expected + (1 if valid is None else jnp.where(valid, 1, 0))
    def columns(group, h):
        return pl.ds(pl.multiple_of((group * heads + h) * DH, DH), DH)

    def part(group):
        return pl.ds(pl.multiple_of(group * rows, rows), rows)

    ins = (k_ref, v_ref, q_ref, g_ref)

    def remote(src, dst, send, recv, device):
        return pltpu.make_async_remote_copy(
            src_ref=src, dst_ref=dst, send_sem=send, recv_sem=recv, device_id=device, device_id_type=MESH
        )

    def landing(h, p):
        return win.at[h, 0, 0, :, part(z), :] if p == 0 else qg.at[h, :, part(z), :]

    def stage_copy(h, a, d):
        return pltpu.make_async_copy(ins[a].at[:, columns(flip(z, d), h)], stage.at[h, a // 2, d - 1, a % 2], st_s.at[h, a, d])

    def local_copy(h, a):
        return pltpu.make_async_copy(ins[a].at[:, columns(z, h)], landing(h, a // 2).at[a % 2], lo_s.at[h, a])

    def in_copy(h, p, d):
        return remote(stage.at[h, p, d - 1], landing(h, p), in_s.at[h, p, d], in_r.at[h, p, d], {"head": flip(z, d)})

    def out_copy(h, p, d, peer=None):
        peer = flip(z, d) if peer is None else peer
        return remote(
            outb.at[h, pl.ds(2 * p, 2), part(peer), :],
            out_ref.at[pl.ds(2 * p, 2), :, columns(z, h)],
            ou_s.at[h, p, d],
            ou_r.at[h, p, d],
            {"head": peer},
        )

    def pair_copy(h, a):
        return remote(win.at[h, 0, 0, a], win.at[h, 0, 1, a], px_s.at[h, a], px_r.at[h, a], {"ta": pair})

    def across_copy(h, a):
        return remote(win.at[h, 0, 1 if relay else 0, a], win.at[h, 0, 2, a], py_s.at[h, a], py_r.at[h, a], {"ta": across})

    def side_copy(h, i, t):
        peer, _, there = sides[i]
        return remote(win.at[h, 0, t], win.at[h, there, t], hc_s.at[h, i, t], hc_r.at[h, there - 1, t], {"ha": peer})

    def back_side(h, i, t):
        peer, _, there = sides[i]
        return remote(r1s.at[h, i, t], r1r.at[h, there - 1, t], bc_s.at[h, i, t], bc_r.at[h, there - 1, t], {"ha": peer})

    def back_pair(h, a):
        return remote(r2s.at[h, 0, a], r2r.at[h, 0, a], bx_s.at[h, a], bx_r.at[h, a], {"ta": pair})

    def back_across(h, a):
        return remote(r2s.at[h, 1, a], r2r.at[h, 1, a], by_s.at[h, a], by_r.at[h, a], {"ta": across})

    def from_side(h, i, t):
        peer = sides[i][0]
        return remote(win.at[h, i + 1, t], win.at[h, i + 1, t], hc_r.at[h, i, t], hc_r.at[h, i, t], {"ha": peer})

    def back_from_side(h, i, t):
        peer = sides[i][0]
        return remote(r1r.at[h, i, t], r1r.at[h, i, t], bc_r.at[h, i, t], bc_r.at[h, i, t], {"ha": peer})

    def both(valid, other):
        return other if valid is None else valid & other

    def send_in(h, p):
        for d in hops:
            for a in (2 * p, 2 * p + 1):
                stage_copy(h, a, d).wait()
            in_copy(h, p, d).start()

    def send_kv(h):
        send_in(h, 0)

    def send_qg(h):
        send_in(h, 1)

    def send_step(h, p, i):
        peer = jnp.where(z == 0, size_z - 1 - i, jnp.where(i >= z, i + 1, i))
        out_copy(h, p, differ(z, peer, size_z), peer).start()

    def send_out(h, p):
        for i in range(size_z - 1):
            send_step(h, p, i)

    def send_ahead(h, p):
        send_step(h, p, 0)

        @pl.when(z == 0)
        def _():
            for i in range(1, size_z - 1):
                send_step(h, p, i)

    def send_kept(h, p):
        pl.when(corner)(lambda: send_ahead(h, p))
        pl.when(inner)(lambda: send_out(h, p))

    def send_rest(h, p):
        @pl.when(z != 0)
        def _():
            for i in range(1, size_z - 1):
                send_step(h, p, i)

    def fetch(h, p):
        for a in (2 * p, 2 * p + 1):
            for d in hops:
                stage_copy(h, a, d).start()
        for a in (2 * p, 2 * p + 1):
            local_copy(h, a).start()

    fetch(0, 0)
    pl.semaphore_wait(barrier, expected)
    send_kv(0)
    if heads > 1:
        fetch(1, 0)
    fetch(0, 1)
    if heads > 1:
        send_kv(1)
    send_qg(0)
    for h in range(2, heads):
        fetch(h, 0)
    for h in range(1, heads):
        fetch(h, 1)

    @pl.when(corner)
    def _():
        @pl.loop(0, heads)
        def _(h):
            for r in range(nr):
                win[h, r, 2] = jnp.zeros((2, tokens, DH), win.dtype)

    for i, (peer, valid, _) in enumerate(sides):
        if valid is not None:

            @pl.when(jnp.logical_not(valid))
            def _(i=i):
                @pl.loop(0, heads)
                def _(h):
                    win[h, i + 1] = jnp.zeros((nt, 2, tokens, DH), win.dtype)


    def to_sides(h, t, cond=None):
        for i, (peer, valid, _) in enumerate(sides):
            go = valid if cond is None else both(valid, cond)
            guarded(go, lambda i=i: side_copy(h, i, t).start())

    def spread_own(h):
        for d in hops:
            in_copy(h, 0, d).wait_recv()
        for a in range(2):
            local_copy(h, a).wait()
            pair_copy(h, a).start()
            if not relay:
                pl.when(inner)(lambda a=a: across_copy(h, a).start())
        to_sides(h, 0)

    def spread_pair(h):
        for a in range(2):
            pair_copy(h, a).wait_recv()
            if relay:
                pl.when(corner)(lambda a=a: across_copy(h, a).start())
        to_sides(h, 1)

    def spread_across(h):
        @pl.when(inner)
        def _():
            for a in range(2):
                across_copy(h, a).wait_recv()
            to_sides(h, 2)

    def score(h):
        for d in hops:
            in_copy(h, 1, d).wait_recv()
        for a in range(2, 4):
            local_copy(h, a).wait()
        queries = qg[h, 0]
        highest = jnp.full((1, tokens), LOW, jnp.float32)
        for r in range(nr):
            for t in range(nt):
                if r > 0:
                    valid = sides[r - 1][1]
                    guarded(both(valid, inner) if t == 2 else valid, lambda r=r, t=t: from_side(h, r - 1, t).wait_recv())
                scores = lax.dot_general(win[h, r, t, 0], queries, (((1,), (1,)), ((), ())), preferred_element_type=jnp.float32) * scale
                for cond in ([inner] if t == 2 else []) + ([sides[r - 1][1]] if r > 0 else []):
                    if cond is not None:
                        scores = jnp.where(cond, scores, LOW)
                s_ref[r * nt + t] = scores
                highest = jnp.maximum(highest, jnp.max(scores, axis=0, keepdims=True))
        return highest

    def forward(h, highest):
        grads = qg[h, 1]
        total = jnp.zeros((1, tokens), jnp.float32)
        mixed = jnp.zeros((DH, tokens), jnp.float32)
        for r in range(nr):
            for t in range(nt):
                weights = jnp.exp2(s_ref[r * nt + t] - highest)
                s_ref[r * nt + t] = weights
                total = total + jnp.sum(weights, axis=0, keepdims=True)
                mixed = mixed + lax.dot_general(
                    win[h, r, t, 1], weights.astype(jnp.bfloat16), (((0,), (0,)), ((), ())), preferred_element_type=jnp.float32
                )
        inverse = 1.0 / total
        attended = jnp.transpose(mixed * inverse).astype(jnp.bfloat16)
        outb[h, 0] = attended
        products = grads.astype(jnp.float32) * attended.astype(jnp.float32)
        row_dot = jnp.sum(jnp.transpose(products), axis=0, keepdims=True)
        return inverse, row_dot

    def fold_sides(h, t):
        for i, (peer, valid, _) in enumerate(sides):

            def fold(i=i, t=t):
                back_from_side(h, i, t).wait_recv()
                own[h, t] = own[h, t] + r1r[h, i, t].astype(jnp.float32)

            guarded(both(valid, inner) if t == 2 else valid, fold)
        if t > 0:

            def send(t=t):
                for a in range(2):
                    r2s[h, t - 1, a] = own[h, t, a].astype(jnp.bfloat16)
                    (back_across if t == 2 else back_pair)(h, a).start()

            guarded(inner if relay or t == 2 else None, send)

    def backward(h, inverse, row_dot, query_grad, rs):
        queries = qg[h, 0]
        grads = qg[h, 1]
        for r in rs:
            for t in reversed(range(nt)):
                keys, values = win[h, r, t, 0], win[h, r, t, 1]
                probs = s_ref[r * nt + t] * inverse
                value_term = jnp.dot(probs.astype(jnp.bfloat16), grads, preferred_element_type=jnp.float32)
                prob_grad = lax.dot_general(values, grads, (((1,), (1,)), ((), ())), preferred_element_type=jnp.float32)
                score_grad = (probs * (prob_grad - row_dot)).astype(jnp.bfloat16)
                query_grad = query_grad + lax.dot_general(
                    keys, score_grad, (((0,), (0,)), ((), ())), preferred_element_type=jnp.float32
                )
                key_term = jnp.dot(score_grad, queries, preferred_element_type=jnp.float32) * factor
                if r == 0:
                    own[h, t, 0] = key_term
                    own[h, t, 1] = value_term
                    fold_sides(h, t)
                else:
                    r1s[h, r - 1, t, 0] = key_term.astype(jnp.bfloat16)
                    r1s[h, r - 1, t, 1] = value_term.astype(jnp.bfloat16)
                    valid = sides[r - 1][1]
                    guarded(both(valid, inner) if t == 2 else valid, lambda r=r, t=t: back_side(h, r - 1, t).start())
        return query_grad

    def send_query_grad(h, query_grad):
        outb[h, 1] = jnp.transpose(query_grad * factor).astype(jnp.bfloat16)
        keep = corner & (h == heads - 1)
        pl.when(keep)(lambda: send_ahead(h, 0))
        pl.when(jnp.logical_not(keep))(lambda: send_out(h, 0))

    def fold_across(h):
        @pl.when(corner if relay else inner)
        def _():
            for a in range(2):
                back_across(h, a).wait_recv()
                if relay:
                    r2s[h, 0, a] = (own[h, 1, a] + r2r[h, 1, a].astype(jnp.float32)).astype(jnp.bfloat16)
                    back_pair(h, a).start()
                else:
                    own[h, 0, a] = own[h, 0, a] + r2r[h, 1, a].astype(jnp.float32)

    def fold_pair(h, send=send_out):
        for a in range(2):
            back_pair(h, a).wait_recv()
            outb[h, a + 2] = (own[h, 0, a] + r2r[h, 0, a].astype(jnp.float32)).astype(jnp.bfloat16)
        send(h, 1)
        for a in range(4):
            out_ref[a, :, columns(z, h)] = outb[h, a, part(z), :]

    def later(h, fn):
        pl.when(h < heads)(lambda: fn(h))

    def earlier(h, fn):
        pl.when(h >= 0)(lambda: fn(h))

    spread_own(0)
    if heads > 2:
        send_kv(2)
    if heads > 1:
        spread_own(1)
        send_qg(1)
    spread_pair(0)
    spread_across(0)

    @pl.loop(0, heads)
    def _(h):
        highest = score(h)
        later(h + 3, send_kv)
        later(h + 1, spread_pair)
        inverse, row_dot = forward(h, highest)
        earlier(h - 2, fold_pair)
        later(h + 2, spread_own)
        later(h + 2, send_qg)
        query_grad = backward(h, inverse, row_dot, jnp.zeros((DH, tokens), jnp.float32), range(nr - 1, 0, -1))
        earlier(h - 1, fold_across)
        query_grad = backward(h, inverse, row_dot, query_grad, (0,))
        send_query_grad(h, query_grad)
        later(h + 1, spread_across)

    final = range(max(0, heads - 2), heads)
    if heads > 1:
        fold_pair(heads - 2, send_kept)
    fold_across(heads - 1)
    fold_pair(heads - 1, send_kept)
    @pl.when(corner)
    def _():
        send_rest(heads - 1, 0)
        for h in final:
            send_rest(h, 1)

    @pl.loop(0, heads)
    def _(h):
        for p in range(2):
            for d in hops:
                in_copy(h, p, d).wait_send()
                out_copy(h, p, d).wait_recv()
                out_copy(h, p, d).wait_send()
        for a in range(2):
            pair_copy(h, a).wait_send()
            back_pair(h, a).wait_send()
            pl.when(corner if relay else inner)(lambda a=a: across_copy(h, a).wait_send())
            pl.when(inner)(lambda a=a: back_across(h, a).wait_send())
        for i, (peer, valid, _) in enumerate(sides):
            for t in range(nt):

                def drain(i=i, t=t):
                    side_copy(h, i, t).wait_send()
                    back_side(h, i, t).wait_send()

                guarded(both(valid, inner) if t == 2 else valid, drain)


def store(held, *refs):
    sems = refs[4]
    copies = [pltpu.make_async_copy(held.at[i], refs[i], sems.at[i]) for i in range(4)]
    for copy in copies:
        copy.start()
    for copy in copies:
        copy.wait()


def body(queries, keys, values, out_grad):
    sizes = tuple(lax.axis_size(axis) for axis in ("ta", "ha", "head"))
    size_t, size_h, size_z = sizes
    assert size_t % 2 == 0 and size_z & (size_z - 1) == 0
    shape = queries.shape
    rows = shape[0] * shape[1] * shape[2]
    width = shape[3]
    heads = width // DH // size_z
    tokens = rows * size_z
    nt, nr = 3, min(3, size_h)
    bf16 = jnp.bfloat16
    dma = pltpu.SemaphoreType.DMA
    mr = max(1, nr - 1)
    flat = [x.reshape(rows, width) for x in (queries, keys, values, out_grad)]
    held = pl.pallas_call(
        functools.partial(kernel, sizes, rows, heads),
        out_shape=pltpu.VMEM((4, rows, width), bf16),
        in_specs=[pl.BlockSpec(memory_space=pl.ANY)] * 4,
        out_specs=pl.BlockSpec(memory_space=pltpu.VMEM),
        scratch_shapes=[
            pltpu.VMEM((heads, 2, tokens, DH), bf16),
            pltpu.VMEM((heads, nr, nt, 2, tokens, DH), bf16),
            pltpu.VMEM((heads, 2, size_z - 1, 2, rows, DH), bf16),
            pltpu.VMEM((nr * nt, tokens, tokens), jnp.float32),
            pltpu.VMEM((heads, 4, tokens, DH), bf16),
            pltpu.VMEM((heads, nt, 2, tokens, DH), jnp.float32),
            pltpu.VMEM((heads, mr, nt, 2, tokens, DH), bf16),
            pltpu.VMEM((heads, mr, nt, 2, tokens, DH), bf16),
            pltpu.VMEM((heads, 2, 2, tokens, DH), bf16),
            pltpu.VMEM((heads, 2, 2, tokens, DH), bf16),
            dma((heads, 2, size_z)),
            dma((heads, 2, size_z)),
            dma((heads, 2)),
            dma((heads, 2)),
            dma((heads, 2)),
            dma((heads, 2)),
            dma((heads, mr, nt)),
            dma((heads, mr, nt)),
            dma((heads, mr, nt)),
            dma((heads, mr, nt)),
            dma((heads, 2)),
            dma((heads, 2)),
            dma((heads, 2)),
            dma((heads, 2)),
            dma((heads, 2, size_z)),
            dma((heads, 2, size_z)),
            dma((heads, 4)),
            dma((heads, 4, size_z)),
        ],
        compiler_params=pltpu.CompilerParams(collective_id=0, has_side_effects=True, vmem_limit_bytes=56 * 1024 * 1024),
        name="tile_attention",
    )(*flat)
    outs = pl.pallas_call(
        store,
        out_shape=[jax.ShapeDtypeStruct((rows, width), bf16)] * 4,
        in_specs=[pl.BlockSpec(memory_space=pl.ANY)],
        out_specs=[pl.BlockSpec(memory_space=pl.ANY)] * 4,
        scratch_shapes=[dma((4,))],
        name="store",
    )(pltpu.with_memory_space_constraint(held, pltpu.VMEM))
    return tuple(x.reshape(shape) for x in outs)


def solution(mesh):
    spec = P("ta", ("ha", "head"), None, None)
    return jax.shard_map(body, mesh=mesh, in_specs=(spec,) * 4, out_specs=(spec,) * 4, check_vma=False)
```
